32 devices in a mesh: seg: 2 (over y), samp: 4 (over x, core), var: 4 (over z).
Axes of the slice: x: 2, y: 2, z: 4, core: 2. Of those that a mesh axis runs over, the one named last changes fastest.
Arguments:
- dosage: bfloat16 [8192, 4096], P('samp', ('seg', 'var')), parts along dimension 1
- observed: int32 [8, 8192], P(('seg', 'var'), 'samp'), parts along dimension 0, may hold values from 0 to 1, as said below
- band_reach: int32 [8], P(('seg', 'var')), parts along dimension 0, may hold values from 0 to 2
Outputs:
- ld_blocks: float32 [8, 512, 3, 512], P(('seg', 'var'), 'samp'), parts along dimension 0
The draws below stay inside these ranges and needn't reach their ends.
There are 2 independent parts, one for each index of `seg`. The reference program is written for one: setup_inputs(seed, part) draws one part's arguments, and reference() takes and returns one part's arrays. A program takes and returns all parts, laid end to end along the dimension named above; each array names one. Nothing has to cross between parts.
Inputs may be any that keep to these rules, and one draw needn't show every extreme that they name: observed is 0 or 1 for each variant block of each individual; every block is observed for at least one individual.
All inputs are finite; a program needn't handle non-finite values.
Results may differ from the reference program's by a relative error of at most 0.0011.
Values may be sent and summed in bfloat16 or wider, within the bound.
No kernel may reach another device: no remote copies, remote signals or barrier semaphores. Data moves between devices by JAX's collectives and lax.ppermute only.
A program may use at most 64 MiB of HBM per device.

```python
import jax
import jax.numpy as jnp
from jax import lax

BLOCK = 512
BAND = 3
SAMPLES = 8192
NBLK = 4
VARIANTS = 2048


def draw_dosage(key, part):
    first_key, second_key = jax.random.split(key, 2)
    noise = jax.random.normal(first_key, (SAMPLES, VARIANTS), jnp.float32)
    mixed = noise + 0.7 * jnp.roll(noise, 1, axis=1) + 0.6 * jnp.roll(noise, BLOCK + 5, axis=1) + 0.5 * jnp.roll(noise, 2 * BLOCK + 37, axis=1)
    frequency = jnp.exp(jax.random.uniform(second_key, (VARIANTS,), jnp.float32, jnp.log(0.05), jnp.log(0.5)))
    logits = jnp.log(frequency / (1.0 - frequency))
    return (2.0 * jax.nn.sigmoid(logits[None, :] + 0.8 * mixed)).astype(jnp.bfloat16)


def disjoint_block(key):
    return jax.random.randint(jax.random.fold_in(key, 11), (), 0, NBLK - 1)


def draw_observed(key, part):
    chosen = disjoint_block(key)
    draws = jax.random.randint(jax.random.fold_in(key, 3), (NBLK, SAMPLES), 0, 1000)
    limit = 300 + 600 * jnp.arange(SAMPLES, dtype=jnp.int32) // SAMPLES
    base = draws < limit[None, :]
    index = jnp.arange(SAMPLES, dtype=jnp.int32)
    blocks = jnp.arange(NBLK, dtype=jnp.int32)
    first_half = index < SAMPLES // 2
    keep_first = jnp.where(blocks[:, None] == chosen, first_half[None, :], True)
    keep_second = jnp.where(blocks[:, None] == chosen + 1, jnp.logical_not(first_half)[None, :], True)
    masked = base & keep_first & keep_second
    forced = jnp.where(blocks[:, None] == chosen + 1, index[None, :] == SAMPLES - 1, index[None, :] == 0)
    return (masked | forced).astype(jnp.int32)


def draw_band_reach(key, part):
    chosen = disjoint_block(key)
    reach = jax.random.randint(jax.random.fold_in(key, 5), (NBLK,), 0, BAND)
    blocks = jnp.arange(NBLK, dtype=jnp.int32)
    return jnp.where(blocks == chosen, BAND - 1, reach).astype(jnp.int32)


def setup_inputs(seed: int = 0, part: int = 0) -> dict:
    streams_of = jax.random.split(jax.random.key(seed), 4)
    part_splits = jax.random.split(jax.random.fold_in(streams_of[3], part), 4)
    dosage = draw_dosage(jax.random.fold_in(jax.random.fold_in(streams_of[3], part), 71), part)
    observed = draw_observed(jax.random.fold_in(jax.random.fold_in(streams_of[3], part), 71), part)
    band_reach = draw_band_reach(jax.random.fold_in(jax.random.fold_in(streams_of[3], part), 71), part)
    return {"dosage": dosage, "observed": observed, "band_reach": band_reach}


EPSILON = 1e-05

def reference(dosage, observed, band_reach):
    blocks = VARIANTS // BLOCK
    weights = observed.astype(jnp.float32)
    values = dosage.astype(jnp.float32).reshape(SAMPLES, blocks, BLOCK)
    totals = lax.optimization_barrier(jnp.sum(weights, axis=1))
    first = jnp.einsum('bs,sbj->bj', weights, values, precision=lax.Precision.HIGHEST)
    second = jnp.einsum('bs,sbj->bj', weights, values * values, precision=lax.Precision.HIGHEST)
    centre = first / totals[:, None]
    spread_inverse = 1.0 / jnp.sqrt(second / totals[:, None] - centre * centre + EPSILON)
    standard = (weights.T[:, :, None] * (values - centre[None]) * spread_inverse[None]).astype(jnp.bfloat16)
    standard_pad = jnp.concatenate([standard, jnp.zeros((SAMPLES, BAND - 1, BLOCK), jnp.bfloat16)], axis=1)
    weights_pad = jnp.concatenate([weights, jnp.zeros((BAND - 1, SAMPLES), jnp.float32)], axis=0)

    def one_block(index):
        own = lax.dynamic_index_in_dim(standard_pad, index, 1, keepdims=False)
        partners = lax.dynamic_slice_in_dim(standard_pad, index, BAND, 1).reshape(SAMPLES, BAND * BLOCK)
        cross = jnp.dot(own.T, partners, preferred_element_type=jnp.float32)
        own_weights = lax.dynamic_index_in_dim(weights_pad, index, 0, keepdims=False)
        band_weights = lax.dynamic_slice_in_dim(weights_pad, index, BAND, 0)
        intersections = jnp.dot(band_weights, own_weights, precision=lax.Precision.HIGHEST)
        keep = jnp.arange(BAND, dtype=jnp.int32) <= lax.dynamic_index_in_dim(band_reach, index, 0, keepdims=False)
        ratio = cross.reshape(BLOCK, BAND, BLOCK) / jnp.maximum(intersections, 1.0)[None, :, None]
        return jnp.where(keep[None, :, None], ratio, jnp.float32(0.0))
    return lax.map(one_block, jnp.arange(blocks, dtype=jnp.int32))
```

```python
import jax
import jax.numpy as jnp
from jax import lax
from jax.sharding import PartitionSpec as P

BAND = 3


EPSILON = 1e-05


def from_above(shard, axis):
    peers = lax.axis_size(axis)
    return lax.ppermute(shard, axis, [(i, i - 1) for i in range(1, peers)])


def from_below(shard, axis):
    peers = lax.axis_size(axis)
    return lax.ppermute(shard, axis, [(i, i + 1) for i in range(peers - 2)])


def swap(shard, axis, bit):
    peers = lax.axis_size(axis)
    return lax.ppermute(shard, axis, [(i, i ^ bit) for i in range(peers)])


def sum_all(value, axis):
    bit = 1
    while bit < lax.axis_size(axis):
        value = value + swap(value, axis, bit)
        bit *= 2
    return value


def sum_rows(partial, axis):
    peers = lax.axis_size(axis)
    place = lax.axis_index(axis)
    rows, columns = partial.shape
    bit = 1
    partial = partial.reshape(peers, rows // peers, columns)
    while bit < peers:
        pairs = partial.reshape(partial.shape[0] // 2, 2, *partial.shape[1:])
        high = (place & bit) != 0
        keep = jnp.where(high, pairs[:, 1], pairs[:, 0])
        give = jnp.where(high, pairs[:, 0], pairs[:, 1])
        partial = keep + swap(give, axis, bit)
        bit *= 2
    return partial[0]


def finish_moments(totals, first_sum, second_sum):
    centre = first_sum / totals
    spread_inverse = 1.0 / jnp.sqrt(second_sum / totals - centre * centre + EPSILON)
    return (centre, spread_inverse)


def standardize(values, weights, centre, spread_inverse):
    return (
        weights[:, None] * (values.astype(jnp.float32) - centre[None, :]) * spread_inverse[None, :]
    ).astype(jnp.bfloat16)


def cross(left, right):
    return lax.dot_general(
        left, right, (((0,), (0,)), ((), ())), preferred_element_type=jnp.float32
    )


def per_device(dosage, observed, band_reach):
    width = dosage.shape[1]
    flags = observed[0].astype(jnp.bfloat16)
    above_flags = from_above(flags, "var")
    below_flags = from_below(flags, "var")
    above = from_above(dosage, "var")
    below = from_below(dosage, "var")
    weights = observed[0].astype(jnp.float32)
    above_weights = above_flags.astype(jnp.float32)
    below_weights = below_flags.astype(jnp.float32)
    first_sum = jnp.dot(flags[None, :], dosage, preferred_element_type=jnp.float32)
    second_sum = jnp.sum(weights[:, None] * jnp.square(dosage.astype(jnp.float32)), axis=0)
    counts = jnp.stack(
        [jnp.sum(weights), jnp.sum(weights * above_weights), jnp.sum(below_weights * above_weights)]
    )
    sums = jnp.concatenate(
        [first_sum, second_sum[None, :], jnp.broadcast_to(counts[:, None], (3, width))], axis=0
    )
    sums = sum_all(sums, "samp")
    totals = sums[2]
    shares = jnp.maximum(sums[2:5], 1.0)
    centre, spread_inverse = finish_moments(totals, sums[0], sums[1])
    moments = jnp.stack([centre, spread_inverse])
    above_moments = from_above(moments, "var")
    below_moments = from_below(moments, "var")
    own = standardize(dosage, weights, centre, spread_inverse)
    same = sum_rows(cross(own, own), "samp") / shares[0]
    above_standard = standardize(above, above_weights, above_moments[0], above_moments[1])
    below_standard = standardize(below, below_weights, below_moments[0], below_moments[1])
    far = sum_rows(cross(below_standard, above_standard), "samp") / shares[2]
    far = from_above(far, "var")
    near = sum_rows(cross(own, above_standard), "samp") / shares[1]
    result = jnp.stack([same, near, far], axis=1)
    keep = jnp.arange(BAND, dtype=jnp.int32) <= band_reach[0]
    return jnp.where(keep[None, :, None], result, jnp.float32(0.0))[None]


def solution(mesh):
    return jax.shard_map(
        per_device,
        mesh=mesh,
        in_specs=(P("samp", ("seg", "var")), P(("seg", "var"), "samp"), P(("seg", "var"))),
        out_specs=P(("seg", "var"), "samp", None, None),
        check_vma=False,
    )
```

```python
import jax
import jax.numpy as jnp
import numpy as np
from jax import lax
from jax.experimental import pallas as pl
from jax.experimental.pallas import tpu as pltpu
from jax.sharding import PartitionSpec as P

BAND = 3


EPSILON = 1e-05

HOLE = float("nan")


def from_above(shard, axis):
    peers = lax.axis_size(axis)
    return lax.ppermute(shard, axis, [(i, i - 1) for i in range(1, peers)])


def from_below(shard, axis):
    peers = lax.axis_size(axis)
    return lax.ppermute(shard, axis, [(i, i + 1) for i in range(peers - 2)])


def swap(shard, axis, bit):
    peers = lax.axis_size(axis)
    return lax.ppermute(shard, axis, [(i, i ^ bit) for i in range(peers)])


def bits_of(peers):
    return [1 << k for k in range(peers.bit_length() - 1)]


def sum_all(value, axis):
    for bit in bits_of(lax.axis_size(axis)):
        value = value + swap(value, axis, bit)
    return value


def sum_rows(partial, axis):
    place = lax.axis_index(axis)
    for bit in bits_of(lax.axis_size(axis)):
        pairs = partial.reshape(partial.shape[0] // 2, 2, *partial.shape[1:])
        high = (place & bit) != 0
        keep = jnp.where(high, pairs[:, 1], pairs[:, 0])
        give = jnp.where(high, pairs[:, 0], pairs[:, 1])
        partial = keep + swap(give, axis, bit)
    return partial[0]


def local(kernel, outs, *args):
    spec = pl.BlockSpec(memory_space=pltpu.VMEM)
    size = sum(int(np.prod(a.shape)) * a.dtype.itemsize for a in (*args, *outs))
    return pl.pallas_call(
        kernel,
        out_shape=tuple(jax.ShapeDtypeStruct(o.shape, o.dtype) for o in outs),
        in_specs=[spec] * len(args),
        out_specs=tuple([spec] * len(outs)),
        cost_estimate=pl.CostEstimate(flops=2 * size, bytes_accessed=size, transcendentals=0),
    )(*args)


def like(shape, dtype):
    return jax.ShapeDtypeStruct(shape, dtype)


def pick(values, order_ref):
    shape = (values.shape[1], order_ref.shape[1])
    chosen = lax.broadcasted_iota(jnp.int32, shape, 0) == order_ref[...]
    return jnp.dot(
        values,
        jnp.where(chosen, 1.0, 0.0).astype(jnp.bfloat16),
        preferred_element_type=jnp.float32,
    )


def head_kernel(dosage_ref, observed_ref, order_ref, down_ref, up_ref):
    lanes = down_ref.shape[1]
    samples = dosage_ref.shape[0]
    flags = observed_ref[...].astype(jnp.float32)
    present = jnp.transpose(jnp.broadcast_to(flags, (lanes, samples))) > 0.5
    down = dosage_ref[:, :lanes].astype(jnp.float32)
    down_ref[...] = jnp.where(present, down, HOLE).astype(jnp.bfloat16)
    up = pick(dosage_ref[...], order_ref)
    up_ref[...] = jnp.where(present, up, HOLE).astype(jnp.bfloat16)


def moments_kernel(dosage_ref, observed_ref, sums_ref):
    flags = observed_ref[...].astype(jnp.float32)
    rows = jnp.broadcast_to(flags, (8, flags.shape[1])).astype(jnp.bfloat16)
    values = dosage_ref[...]
    exact = values.astype(jnp.float32)
    square = exact * exact
    high = square.astype(jnp.bfloat16)
    low = (square - high.astype(jnp.float32)).astype(jnp.bfloat16)

    def total(part):
        return jnp.dot(rows, part, preferred_element_type=jnp.float32)[:1]

    sums_ref[0:1, :] = total(values)
    sums_ref[1:2, :] = total(high) + total(low)
    count = jnp.sum(flags, axis=1, keepdims=True)
    sums_ref[2:3, :] = jnp.broadcast_to(count, (1, sums_ref.shape[1]))
    sums_ref[3:8, :] = jnp.zeros((5, sums_ref.shape[1]), jnp.float32)


def finish_moments(totals, first_sum, second_sum):
    centre = first_sum / totals
    spread_inverse = 1.0 / jnp.sqrt(second_sum / totals - centre * centre + EPSILON)
    return (centre, spread_inverse)


def own_kernel(dosage_ref, down_ref, sums_ref, order_ref, moments_ref, own_ref, *cut_refs):
    lanes = down_ref.shape[1]
    width = own_ref.shape[1]
    centre, inverse = finish_moments(sums_ref[2:3, :], sums_ref[0:1, :], sums_ref[1:2, :])
    moments_ref[0:1, :] = centre
    moments_ref[1:2, :] = inverse
    moments_ref[2:8, :] = jnp.zeros((6, width), jnp.float32)
    down = down_ref[...].astype(jnp.float32)
    present = down == down
    parts = []
    for low in range(0, width, lanes):
        spread = dosage_ref[:, low : low + lanes].astype(jnp.float32)
        spread = (spread - centre[:, low : low + lanes]) * inverse[:, low : low + lanes]
        parts.append(jnp.where(present, spread, 0.0).astype(jnp.bfloat16))
        own_ref[:, low : low + lanes] = parts[-1]
    half = len(cut_refs) // 2
    low = lanes
    for ref in cut_refs[:half]:
        ref[...] = own_ref[:, low : low + ref.shape[1]]
        low += ref.shape[1]
    up = pick(own_ref[...], order_ref).astype(jnp.bfloat16)
    low = 0
    for ref in cut_refs[half:]:
        ref[...] = up[:, low : low + ref.shape[1]]
        low += ref.shape[1]


def first_kernel(
    own_ref, above_ref, below_ref, above_m_ref, below_m_ref, shares_ref, above_out, below_out
):
    def split(ref):
        values = ref[...].astype(jnp.float32)
        return values, values == values

    def standardize(values, present, moments):
        spread = (values - moments[0:1, :]) * moments[1:2, :]
        return jnp.where(present, spread, 0.0).astype(jnp.bfloat16)

    _, own_present = split(own_ref)
    above, above_present = split(above_ref)
    below, below_present = split(below_ref)
    above_out[...] = standardize(above, above_present, above_m_ref)
    below_out[...] = standardize(below, below_present, below_m_ref)
    above_one = jnp.where(above_present, 1.0, 0.0)
    shares_ref[0:1, :] = jnp.sum(jnp.where(own_present, above_one, 0.0), axis=0, keepdims=True)
    shares_ref[1:2, :] = jnp.sum(jnp.where(below_present, above_one, 0.0), axis=0, keepdims=True)
    shares_ref[2:8, :] = jnp.zeros((6, shares_ref.shape[1]), jnp.float32)


def cross(left, right):
    return lax.dot_general(
        left, right, (((0,), (0,)), ((), ())), preferred_element_type=jnp.float32
    )


def per_device(dosage, observed, band_reach):
    samples, width = dosage.shape
    peers = lax.axis_size("samp")
    rows = width // peers
    row_edges = (0, rows // 4, 3 * rows // 4, rows)
    edges = tuple(edge * peers for edge in row_edges)
    order = np.concatenate(
        [
            (np.arange(peers)[:, None] * rows + np.arange(low, high)[None, :]).ravel()
            for low, high in zip(row_edges[:-1], row_edges[1:])
        ]
    ).astype(np.int32)[None, :]
    first, split, tail = edges[1], row_edges[2], rows - row_edges[2]
    quarters = width // first
    half = jnp.bfloat16
    down_a, up_a = local(
        head_kernel,
        [like((samples, first), half)] * 2,
        dosage,
        observed,
        jnp.asarray(order[:, :first]),
    )
    above_a = from_above(down_a, "var")
    below_a = from_below(up_a, "var")
    (sums,) = local(moments_kernel, [like((8, width), jnp.float32)], dosage, observed)
    sums = sum_all(sums, "samp")
    cuts = [like((samples, edges[2] - edges[1]), half), like((samples, edges[3] - edges[2]), half)]
    moments, own, down_b, down_c, up_b, up_c = local(
        own_kernel,
        [like((8, width), jnp.float32), like((samples, width), half)] + cuts * 2,
        dosage,
        down_a,
        sums,
        jnp.asarray(order[:, first:]),
    )
    above_m = from_above(moments[:, :first], "var")
    below_m = moments.reshape(8, peers, rows)[:, :, : row_edges[1]].reshape(8, first)
    below_m = from_below(below_m, "var")
    above_b = from_above(down_b, "var")
    below_b = from_below(up_b, "var")
    above_c = from_above(down_c, "var")
    below_c = from_below(up_c, "var")
    same = sum_rows(cross(own, own).reshape(peers, rows, width), "samp")
    shares, above_a, below_a = local(
        first_kernel,
        [like((8, first), jnp.float32)] + [like((samples, first), half)] * 2,
        down_a,
        above_a,
        below_a,
        above_m,
        below_m,
    )
    shares = jnp.maximum(sum_all(shares, "samp"), 1.0)
    above_1 = jnp.concatenate([above_a, above_b], axis=1)
    below_1 = jnp.concatenate([below_a, below_b], axis=1)
    near = cross(own, above_1).reshape(peers, rows, edges[2])
    far = cross(below_1, above_1)
    far = [
        far[edges[k] : edges[k + 1]].reshape(peers, row_edges[k + 1] - row_edges[k], edges[2])
        for k in range(2)
    ]
    one = sum_rows(jnp.concatenate([near] + far, axis=1), "samp")
    near_1 = one[:rows]
    far_1 = from_above(one[rows:] / shares[1:2, :1], "var")
    far = cross(below_1, above_c)
    far = [
        far[edges[k] : edges[k + 1]].reshape(peers, row_edges[k + 1] - row_edges[k], first)
        for k in range(2)
    ]
    last = cross(below_c, jnp.concatenate([above_1, above_c], axis=1))
    last = last.reshape(peers, tail, width)
    last = [last[:, :, k * first : (k + 1) * first] for k in range(quarters)]
    two = sum_rows(jnp.concatenate(far + last, axis=1), "samp")
    far_2 = from_above(two / shares[1:2, :1], "var")
    near_2 = sum_rows(cross(own, above_c).reshape(peers, rows, first), "samp")
    near = jnp.concatenate([near_1, near_2], axis=1) / shares[0:1, :1]
    far_2 = jnp.concatenate(
        [
            jnp.concatenate([far_1, far_2[:split]], axis=1),
            jnp.concatenate(
                [far_2[split + k * tail : split + (k + 1) * tail] for k in range(quarters)],
                axis=1,
            ),
        ],
        axis=0,
    )
    result = jnp.stack([same / jnp.maximum(sums[2:3], 1.0), near, far_2], axis=1)
    keep = jnp.arange(BAND, dtype=jnp.int32) <= band_reach[0]
    return jnp.where(keep[None, :, None], result, jnp.float32(0.0))[None]


def solution(mesh):
    return jax.shard_map(
        per_device,
        mesh=mesh,
        in_specs=(P("samp", ("seg", "var")), P(("seg", "var"), "samp"), P(("seg", "var"))),
        out_specs=P(("seg", "var"), "samp", None, None),
        check_vma=False,
    )
```

```python
import jax
import jax.numpy as jnp
import numpy as np
from jax import lax
from jax.experimental import pallas as pl
from jax.sharding import PartitionSpec as P

BAND = 3


EPSILON = 1e-05

HOLE = float("nan")


def from_above(shard, axis):
    peers = lax.axis_size(axis)
    return lax.ppermute(shard, axis, [(i, i - 1) for i in range(1, peers)])


def from_below(shard, axis):
    peers = lax.axis_size(axis)
    return lax.ppermute(shard, axis, [(i, i + 1) for i in range(peers - 2)])


def swap(shard, axis, bit):
    peers = lax.axis_size(axis)
    return lax.ppermute(shard, axis, [(i, i ^ bit) for i in range(peers)])


def bits_of(peers):
    return [1 << k for k in range(peers.bit_length() - 1)]


def sum_all(value, axis):
    for bit in bits_of(lax.axis_size(axis)):
        value = value + swap(value, axis, bit)
    return value


def sum_rows(partial, axis):
    place = lax.axis_index(axis)
    for bit in bits_of(lax.axis_size(axis)):
        pairs = partial.reshape(partial.shape[0] // 2, 2, *partial.shape[1:])
        high = (place & bit) != 0
        keep = jnp.where(high, pairs[:, 1], pairs[:, 0])
        give = jnp.where(high, pairs[:, 0], pairs[:, 1])
        partial = keep + swap(give, axis, bit)
    return partial[0]


def like(shape, dtype):
    return jax.ShapeDtypeStruct(shape, dtype)


def head_kernel(dosage_ref, observed_ref, order_ref, down_1, down_2, up_1, up_2, sums_ref):
    samples, width = dosage_ref.shape
    lanes = 128

    @pl.when(pl.program_id(0) == 0)
    def _():
        sums_ref[...] = jnp.zeros_like(sums_ref)

    flags = observed_ref[...].astype(jnp.float32)
    present = jnp.transpose(jnp.broadcast_to(flags, (lanes, samples))) > 0.5
    count = jnp.sum(jnp.where(present, 1.0, 0.0), axis=0, keepdims=True)
    chosen = lax.broadcasted_iota(jnp.int32, (width, width), 0) == order_ref[...]
    up = jnp.dot(
        dosage_ref[...],
        jnp.where(chosen, 1.0, 0.0).astype(jnp.bfloat16),
        preferred_element_type=jnp.float32,
    )
    edge = down_1.shape[1]
    for low in range(0, width, lanes):
        part = slice(low, low + lanes)
        down = dosage_ref[:, part].astype(jnp.float32)
        kept = jnp.where(present, down, 0.0)
        sums_ref[0:1, part] += jnp.sum(kept, axis=0, keepdims=True)
        sums_ref[1:2, part] += jnp.sum(kept * kept, axis=0, keepdims=True)
        sums_ref[2:3, part] += count
        down = jnp.where(present, down, HOLE).astype(jnp.bfloat16)
        coded = jnp.where(present, up[:, part], HOLE).astype(jnp.bfloat16)
        if low < edge:
            down_1[:, part] = down
            up_1[:, part] = coded
        else:
            down_2[:, low - edge : low - edge + lanes] = down
            up_2[:, low - edge : low - edge + lanes] = coded


def head(dosage, observed, order, edge):
    samples, width = dosage.shape
    block = 256 if samples % 256 == 0 else samples
    cuts = [edge, width - edge] * 2
    return pl.pallas_call(
        head_kernel,
        grid=(samples // block,),
        out_shape=tuple(like((samples, cut), jnp.bfloat16) for cut in cuts)
        + (like((8, width), jnp.float32),),
        in_specs=[
            pl.BlockSpec((block, width), lambda i: (i, 0)),
            pl.BlockSpec((1, block), lambda i: (0, i)),
            pl.BlockSpec((1, width), lambda i: (0, 0)),
        ],
        out_specs=tuple(pl.BlockSpec((block, cut), lambda i: (i, 0)) for cut in cuts)
        + (pl.BlockSpec((8, width), lambda i: (0, 0)),),
        name="head",
    )(dosage, observed, order)


def finish_moments(sums):
    centre = sums[0:1] / sums[2:3]
    spread_inverse = 1.0 / jnp.sqrt(sums[1:2] / sums[2:3] - centre * centre + EPSILON)
    return jnp.concatenate([centre, spread_inverse], axis=0)


def standardize(values, present, moments):
    spread = (values.astype(jnp.float32) - moments[0:1]) * moments[1:2]
    return lax.optimization_barrier(jnp.where(present, spread, 0.0).astype(jnp.bfloat16))


def cross(left, right):
    return lax.dot_general(
        left, right, (((0,), (0,)), ((), ())), preferred_element_type=jnp.float32
    )


def per_device(dosage, observed, band_reach):
    _, width = dosage.shape
    peers = lax.axis_size("samp")
    rows = width // peers
    kept = 3 * rows // 4
    tail = rows - kept
    edge, rest = kept * peers, tail * peers
    owners = np.arange(peers)[:, None] * rows
    order = np.concatenate(
        [
            (owners + np.arange(0, kept)[None, :]).ravel(),
            (owners + np.arange(kept, rows)[None, :]).ravel(),
        ]
    ).astype(np.int32)[None, :]
    pieces = width // rest
    down_1, down_2, up_1, up_2, sums = head(dosage, observed, jnp.asarray(order), edge)
    above_1 = from_above(down_1, "var")
    below_1 = from_below(up_1, "var")
    sums = sum_all(sums, "samp")
    moments = finish_moments(sums)
    above_m = from_above(moments, "var")
    below_m = from_below(moments, "var")
    above_2 = from_above(down_2, "var")
    below_2 = from_below(up_2, "var")
    own = standardize(dosage, (observed[0] != 0)[:, None], moments)
    same = sum_rows(cross(own, own).reshape(peers, rows, width), "samp")
    below_m = below_m.reshape(2, peers, rows)
    below_m1 = below_m[:, :, :kept].reshape(2, edge)
    below_m2 = below_m[:, :, kept:].reshape(2, rest)
    own_present = jnp.logical_not(jnp.isnan(down_1))
    above_present = jnp.logical_not(jnp.isnan(above_1))
    below_present = jnp.logical_not(jnp.isnan(below_1))
    above_1 = standardize(above_1, above_present, above_m[:, :edge])
    below_1 = standardize(below_1, below_present, below_m1)
    shares = [
        jnp.sum(jnp.where(other & above_present, 1.0, 0.0), axis=0, keepdims=True)
        for other in (own_present, below_present)
    ]
    shares = jnp.concatenate(shares + [jnp.zeros((6, edge), jnp.float32)], axis=0)
    near = cross(own, above_1).reshape(peers, rows, edge)
    far = cross(below_1, above_1).reshape(peers, kept, edge)
    shares = jnp.broadcast_to(shares[None], (peers, 8, edge))
    one = sum_rows(jnp.concatenate([near, far, shares], axis=1), "samp")
    shares = jnp.maximum(one[rows + kept :], 1.0)
    near_1 = one[:rows] / shares[0:1]
    far_1 = one[rows : rows + kept] / shares[1:2]
    far_1 = from_above(far_1, "var")
    above_2 = standardize(above_2, jnp.logical_not(jnp.isnan(above_2)), above_m[:, edge:])
    below_2 = standardize(below_2, jnp.logical_not(jnp.isnan(below_2)), below_m2)
    far = cross(below_1, above_2).reshape(peers, kept, rest)
    last = [cross(below_2, above_1), cross(below_2, above_2)]
    last = [part.reshape(peers, tail, part.shape[1]) for part in last]
    last = [last[0][:, :, k * rest : (k + 1) * rest] for k in range(pieces - 1)] + [last[1]]
    two = sum_rows(jnp.concatenate([far] + last, axis=1), "samp") / shares[1:2, :rest]
    far_2 = from_above(two, "var")
    near_2 = sum_rows(cross(own, above_2).reshape(peers, rows, rest), "samp")
    near_2 = near_2 / shares[0:1, :rest]
    near = jnp.concatenate([near_1, near_2], axis=1)
    low = [far_2[kept + k * tail : kept + (k + 1) * tail] for k in range(pieces)]
    far = jnp.concatenate(
        [
            jnp.concatenate([far_1, far_2[:kept]], axis=1),
            jnp.concatenate(low, axis=1),
        ],
        axis=0,
    )
    result = jnp.stack([same / jnp.maximum(sums[2:3], 1.0), near, far], axis=1)
    keep = jnp.arange(BAND, dtype=jnp.int32) <= band_reach[0]
    return jnp.where(keep[None, :, None], result, jnp.float32(0.0))[None]


def solution(mesh):
    return jax.shard_map(
        per_device,
        mesh=mesh,
        in_specs=(P("samp", ("seg", "var")), P(("seg", "var"), "samp"), P(("seg", "var"))),
        out_specs=P(("seg", "var"), "samp", None, None),
        check_vma=False,
    )
```

```python
import jax
import jax.numpy as jnp
import numpy as np
from jax import lax
from jax.experimental import pallas as pl
from jax.experimental.pallas import tpu as pltpu
from jax.sharding import PartitionSpec as P

BAND = 3


EPSILON = 1e-05

HOLE = float("nan")


def from_above(shard, axis):
    peers = lax.axis_size(axis)
    return lax.ppermute(shard, axis, [(i, i - 1) for i in range(1, peers)])


def from_below(shard, axis):
    peers = lax.axis_size(axis)
    return lax.ppermute(shard, axis, [(i, i + 1) for i in range(peers - 2)])


def swap(shard, axis, bit):
    peers = lax.axis_size(axis)
    return lax.ppermute(shard, axis, [(i, i ^ bit) for i in range(peers)])


def bits_of(peers):
    return [1 << k for k in range(peers.bit_length() - 1)]


def sum_all(value, axis):
    for bit in bits_of(lax.axis_size(axis)):
        value = value + swap(value, axis, bit)
    return value


def sum_rows(partial, axis):
    place = lax.axis_index(axis)
    for bit in bits_of(lax.axis_size(axis)):
        pairs = partial.reshape(partial.shape[0] // 2, 2, *partial.shape[1:])
        high = (place & bit) != 0
        keep = jnp.where(high, pairs[:, 1], pairs[:, 0])
        give = jnp.where(high, pairs[:, 0], pairs[:, 1])
        partial = keep + swap(give, axis, bit)
    return partial[0]


GRANT = 20 << 20


def block_of(samples):
    return 512 if samples % 512 == 0 else samples


def in_hbm(array):
    return pltpu.with_memory_space_constraint(array, pltpu.HBM)


def like(shape, dtype):
    return jax.ShapeDtypeStruct(shape, dtype)


def head_kernel(dosage_ref, observed_ref, order_ref, down_1, down_2, up_1, up_2, sums_ref):
    samples, width = dosage_ref.shape
    lanes = 128

    @pl.when(pl.program_id(0) == 0)
    def _():
        sums_ref[...] = jnp.zeros_like(sums_ref)

    flags = observed_ref[...].astype(jnp.float32)
    present = jnp.transpose(jnp.broadcast_to(flags, (lanes, samples))) > 0.5
    count = jnp.sum(jnp.where(present, 1.0, 0.0), axis=0, keepdims=True)
    up = jnp.dot(dosage_ref[...], order_ref[...], preferred_element_type=jnp.float32)
    edge = down_1.shape[1]
    for low in range(0, width, lanes):
        part = slice(low, low + lanes)
        down = dosage_ref[:, part].astype(jnp.float32)
        kept = jnp.where(present, down, 0.0)
        sums_ref[0:1, part] += jnp.sum(kept, axis=0, keepdims=True)
        sums_ref[1:2, part] += jnp.sum(kept * kept, axis=0, keepdims=True)
        sums_ref[2:3, part] += count
        down = jnp.where(present, down, HOLE).astype(jnp.bfloat16)
        coded = jnp.where(present, up[:, part], HOLE).astype(jnp.bfloat16)
        if low < edge:
            down_1[:, part] = down
            up_1[:, part] = coded
        else:
            down_2[:, low - edge : low - edge + lanes] = down
            up_2[:, low - edge : low - edge + lanes] = coded


def head(dosage, observed, order, edge):
    samples, width = dosage.shape
    block = block_of(samples)
    cuts = [edge, width - edge] * 2
    return pl.pallas_call(
        head_kernel,
        grid=(samples // block,),
        out_shape=tuple(like((samples, cut), jnp.bfloat16) for cut in cuts)
        + (like((8, width), jnp.float32),),
        in_specs=[
            pl.BlockSpec((block, width), lambda i: (i, 0)),
            pl.BlockSpec((1, block), lambda i: (0, i)),
            pl.BlockSpec((width, width), lambda i: (0, 0)),
        ],
        out_specs=tuple(pl.BlockSpec((block, cut), lambda i: (i, 0)) for cut in cuts)
        + (pl.BlockSpec((8, width), lambda i: (0, 0)),),
        compiler_params=pltpu.CompilerParams(vmem_limit_bytes=GRANT),
        name="head",
    )(in_hbm(dosage), observed, order)


def finish_moments(sums):
    centre = sums[0:1] / sums[2:3]
    spread_inverse = 1.0 / jnp.sqrt(sums[1:2] / sums[2:3] - centre * centre + EPSILON)
    return jnp.concatenate([centre, spread_inverse], axis=0)


def standardize(values, present, moments):
    spread = (values.astype(jnp.float32) - moments[0:1]) * moments[1:2]
    return jnp.where(present, spread, 0.0).astype(jnp.bfloat16)


def decode(ref, moments_ref):
    values = ref[...].astype(jnp.float32)
    spread = (values - moments_ref[0:1, :]) * moments_ref[1:2, :]
    return jnp.where(values == values, spread, 0.0).astype(jnp.bfloat16)


def flags_of(ref):
    values = ref[:, :128].astype(jnp.float32)
    return jnp.where(values == values, 1.0, 0.0)


def cross(left, right):
    return lax.dot_general(
        left, right, (((0,), (0,)), ((), ())), preferred_element_type=jnp.float32
    )


def first_kernel(
    coded_ref, above_ref, below_ref, own_ref, above_m, below_m, out_ref, above_out, below_out
):
    peers, _, edge = out_ref.shape
    rows = own_ref.shape[1] // peers
    kept = edge // peers

    @pl.when(pl.program_id(0) == 0)
    def _():
        out_ref[...] = jnp.zeros_like(out_ref)

    above = decode(above_ref, above_m)
    below = decode(below_ref, below_m)
    above_out[...] = above
    below_out[...] = below
    near = cross(own_ref[...], above)
    far = cross(below, above)
    above_one = flags_of(above_ref)
    shares = [
        jnp.sum(flags_of(ref) * above_one, axis=0, keepdims=True) for ref in (coded_ref, below_ref)
    ]
    for k in range(peers):
        out_ref[k, :rows, :] += near[k * rows : (k + 1) * rows]
        out_ref[k, rows : rows + kept, :] += far[k * kept : (k + 1) * kept]
        for low in range(0, edge, 128):
            out_ref[k, rows + kept : rows + kept + 1, low : low + 128] += shares[0]
            out_ref[k, rows + kept + 1 : rows + kept + 2, low : low + 128] += shares[1]


def first_pass(coded, above, below, own, above_m, below_m, peers):
    samples, width = own.shape
    edge = above.shape[1]
    block = block_of(samples)
    tall = (peers, width // peers + edge // peers + 8, edge)

    def rows_of(cut):
        return pl.BlockSpec((block, cut), lambda i: (i, 0))

    moments = pl.BlockSpec((2, edge), lambda i: (0, 0))
    flops = 2 * samples * edge * (width + edge)
    return pl.pallas_call(
        first_kernel,
        grid=(samples // block,),
        out_shape=(like(tall, jnp.float32),) + (like((samples, edge), jnp.bfloat16),) * 2,
        in_specs=[rows_of(128), rows_of(edge), rows_of(edge), rows_of(width), moments, moments],
        out_specs=(pl.BlockSpec(tall, lambda i: (0, 0, 0)), rows_of(edge), rows_of(edge)),
        compiler_params=pltpu.CompilerParams(vmem_limit_bytes=GRANT),
        cost_estimate=pl.CostEstimate(
            flops=flops, bytes_accessed=12 * samples * edge, transcendentals=0
        ),
        name="first",
    )(coded, above, below, own, above_m, below_m)


def second_kernel(above_ref, below_ref, above_1, below_1, own_ref, above_m, below_m, out_ref):
    peers, _, rest = out_ref.shape
    width, edge = own_ref.shape[1], above_1.shape[1]
    rows, kept, tail = width // peers, edge // peers, rest // peers

    @pl.when(pl.program_id(0) == 0)
    def _():
        out_ref[...] = jnp.zeros_like(out_ref)

    above = decode(above_ref, above_m)
    below = decode(below_ref, below_m)
    near = cross(own_ref[...], above)
    far = cross(below_1[...], above)
    last = cross(below, above_1[...])
    corner = cross(below, above)
    for k in range(peers):
        out_ref[k, :rows, :] += near[k * rows : (k + 1) * rows]
        low = rows + kept
        out_ref[k, rows:low, :] += far[k * kept : (k + 1) * kept]
        for left in range(0, edge, rest):
            out_ref[k, low : low + tail, :] += last[k * tail : (k + 1) * tail, left : left + rest]
            low += tail
        out_ref[k, low : low + tail, :] += corner[k * tail : (k + 1) * tail]


def second_pass(above, below, above_1, below_1, own, above_m, below_m, peers):
    samples, width = own.shape
    edge, rest = above_1.shape[1], above.shape[1]
    block = block_of(samples)
    tall = (peers, (width + edge + width) // peers, rest)

    def rows_of(cut):
        return pl.BlockSpec((block, cut), lambda i: (i, 0))

    moments = pl.BlockSpec((2, rest), lambda i: (0, 0))
    flops = 2 * samples * rest * (2 * width + edge)
    return pl.pallas_call(
        second_kernel,
        grid=(samples // block,),
        out_shape=like(tall, jnp.float32),
        in_specs=[rows_of(rest)] * 2 + [rows_of(edge)] * 2 + [rows_of(width)] + [moments] * 2,
        out_specs=pl.BlockSpec(tall, lambda i: (0, 0, 0)),
        compiler_params=pltpu.CompilerParams(vmem_limit_bytes=GRANT),
        cost_estimate=pl.CostEstimate(
            flops=flops, bytes_accessed=2 * samples * (2 * width + edge), transcendentals=0
        ),
        name="second",
    )(above, below, in_hbm(above_1), in_hbm(below_1), own, above_m, below_m)


def per_device(dosage, observed, band_reach):
    _, width = dosage.shape
    peers = lax.axis_size("samp")
    rows = width // peers
    kept = 3 * rows // 4
    tail = rows - kept
    edge, rest = kept * peers, tail * peers
    owners = np.arange(peers)[:, None] * rows
    order = np.concatenate(
        [
            (owners + np.arange(0, kept)[None, :]).ravel(),
            (owners + np.arange(kept, rows)[None, :]).ravel(),
        ]
    )
    pieces = width // rest
    chosen = jnp.asarray(np.arange(width)[:, None] == order[None, :], jnp.bfloat16)
    down_1, down_2, up_1, up_2, sums = head(dosage, observed, chosen, edge)
    above_1 = from_above(down_1, "var")
    below_1 = from_below(up_1, "var")
    sums = sum_all(sums, "samp")
    moments = finish_moments(sums)
    above_m = from_above(moments, "var")
    below_m = from_below(moments, "var")
    above_2 = from_above(down_2, "var")
    below_2 = from_below(up_2, "var")
    own = standardize(dosage, (observed[0] != 0)[:, None], moments)
    own = lax.optimization_barrier(own)
    same = sum_rows(cross(own, own).reshape(peers, rows, width), "samp")
    below_m = below_m.reshape(2, peers, rows)
    below_m1 = below_m[:, :, :kept].reshape(2, edge)
    below_m2 = below_m[:, :, kept:].reshape(2, rest)
    above_m1, above_m2 = above_m[:, :edge], above_m[:, edge:]
    one, above_1, below_1 = first_pass(
        down_1, above_1, below_1, own, above_m1, below_m1, peers
    )
    one = sum_rows(one, "samp")
    shares = jnp.maximum(one[rows + kept :], 1.0)
    near_1 = one[:rows] / shares[0:1]
    far_1 = one[rows : rows + kept] / shares[1:2]
    far_1 = from_above(far_1, "var")
    two = second_pass(
        above_2, below_2, above_1, below_1, own, above_m2, below_m2, peers
    )
    two = sum_rows(two, "samp")
    far_2 = two[rows:] / shares[1:2, :rest]
    far_2 = from_above(far_2, "var")
    near = jnp.concatenate([near_1, two[:rows] / shares[0:1, :rest]], axis=1)
    low = [far_2[kept + k * tail : kept + (k + 1) * tail] for k in range(pieces)]
    far = jnp.concatenate(
        [
            jnp.concatenate([far_1, far_2[:kept]], axis=1),
            jnp.concatenate(low, axis=1),
        ],
        axis=0,
    )
    result = jnp.stack([same / jnp.maximum(sums[2:3], 1.0), near, far], axis=1)
    keep = jnp.arange(BAND, dtype=jnp.int32) <= band_reach[0]
    return jnp.where(keep[None, :, None], result, jnp.float32(0.0))[None]


def solution(mesh):
    return jax.shard_map(
        per_device,
        mesh=mesh,
        in_specs=(P("samp", ("seg", "var")), P(("seg", "var"), "samp"), P(("seg", "var"))),
        out_specs=P(("seg", "var"), "samp", None, None),
        check_vma=False,
    )
```

```python
import jax
import jax.numpy as jnp
import numpy as np
from jax import lax
from jax.experimental import pallas as pl
from jax.experimental.pallas import tpu as pltpu
from jax.sharding import PartitionSpec as P

BAND = 3


EPSILON = 1e-05


def from_above(shard, axis):
    peers = lax.axis_size(axis)
    return lax.ppermute(shard, axis, [(i, i - 1) for i in range(1, peers)])


def from_below(shard, axis):
    peers = lax.axis_size(axis)
    return lax.ppermute(shard, axis, [(i, i + 1) for i in range(peers - 2)])


def swap(shard, axis, bit):
    peers = lax.axis_size(axis)
    return lax.ppermute(shard, axis, [(i, i ^ bit) for i in range(peers)])


def bits_of(peers):
    return [1 << k for k in range(peers.bit_length() - 1)]


def sum_all(value, axis):
    for bit in bits_of(lax.axis_size(axis)):
        value = value + swap(value, axis, bit)
    return value


def sum_rows(partial, axis):
    place = lax.axis_index(axis)
    for bit in bits_of(lax.axis_size(axis)):
        pairs = partial.reshape(partial.shape[0] // 2, 2, *partial.shape[1:])
        high = (place & bit) != 0
        keep = jnp.where(high, pairs[:, 1], pairs[:, 0])
        give = jnp.where(high, pairs[:, 0], pairs[:, 1])
        partial = keep + swap(give, axis, bit)
    return partial[0]


GRANT = 20 << 20


def block_of(samples):
    return 512 if samples % 512 == 0 else samples


def in_hbm(array):
    return pltpu.with_memory_space_constraint(array, pltpu.HBM)


def like(shape, dtype):
    return jax.ShapeDtypeStruct(shape, dtype)


def mask_of(row):
    lanes = 128
    return jnp.transpose(jnp.broadcast_to(row.astype(jnp.float32), (lanes, row.shape[1]))) > 0.5


def head_kernel(dosage_ref, order_ref, up_ref, down_ref, chosen_ref):
    @pl.when(pl.program_id(0) == 0)
    def _():
        rows = lax.broadcasted_iota(jnp.int32, chosen_ref.shape, 0)
        chosen_ref[...] = jnp.where(rows == order_ref[...], 1.0, 0.0).astype(jnp.bfloat16)

    down_ref[...] = dosage_ref[:, : down_ref.shape[1]]
    up = jnp.dot(dosage_ref[...], chosen_ref[...], preferred_element_type=jnp.float32)
    up_ref[...] = up.astype(jnp.bfloat16)


def head_pass(dosage, order):
    samples, width = dosage.shape
    block, edge = block_of(samples), order.shape[1]
    return pl.pallas_call(
        head_kernel,
        grid=(samples // block,),
        out_shape=(like((samples, edge), jnp.bfloat16),) * 2,
        in_specs=[
            pl.BlockSpec((block, width), lambda i: (i, 0)),
            pl.BlockSpec((1, edge), lambda i: (0, 0)),
        ],
        out_specs=(pl.BlockSpec((block, edge), lambda i: (i, 0)),) * 2,
        scratch_shapes=[pltpu.VMEM((width, edge), jnp.bfloat16)],
        compiler_params=pltpu.CompilerParams(vmem_limit_bytes=GRANT),
        name="head",
    )(in_hbm(dosage), in_hbm(order))


def moments_kernel(dosage_ref, observed_ref, chosen_ref, down_2, up_2, sums_ref):
    width = dosage_ref.shape[1]
    lanes = 128

    @pl.when(pl.program_id(0) == 0)
    def _():
        sums_ref[...] = jnp.zeros_like(sums_ref)

    present = mask_of(observed_ref[...])
    count = jnp.sum(jnp.where(present, 1.0, 0.0), axis=0, keepdims=True)
    for low in range(0, width, lanes):
        part = slice(low, low + lanes)
        kept = jnp.where(present, dosage_ref[:, part].astype(jnp.float32), 0.0)
        sums_ref[0:1, part] += jnp.sum(kept, axis=0, keepdims=True)
        sums_ref[1:2, part] += jnp.sum(kept * kept, axis=0, keepdims=True)
        sums_ref[2:3, part] += count
    down_2[...] = dosage_ref[:, width - down_2.shape[1] :]
    up = jnp.dot(dosage_ref[...], chosen_ref[...], preferred_element_type=jnp.float32)
    up_2[...] = up.astype(jnp.bfloat16)


def moments_pass(dosage, observed, chosen):
    samples, width = dosage.shape
    block, rest = block_of(samples), chosen.shape[1]
    return pl.pallas_call(
        moments_kernel,
        grid=(samples // block,),
        out_shape=(like((samples, rest), jnp.bfloat16),) * 2 + (like((8, width), jnp.float32),),
        in_specs=[
            pl.BlockSpec((block, width), lambda i: (i, 0)),
            pl.BlockSpec((1, block), lambda i: (0, i)),
            pl.BlockSpec((width, rest), lambda i: (0, 0)),
        ],
        out_specs=(pl.BlockSpec((block, rest), lambda i: (i, 0)),) * 2
        + (pl.BlockSpec((8, width), lambda i: (0, 0)),),
        compiler_params=pltpu.CompilerParams(vmem_limit_bytes=GRANT),
        cost_estimate=pl.CostEstimate(
            flops=2 * samples * width * rest,
            bytes_accessed=2 * samples * (width + 2 * rest),
            transcendentals=0,
        ),
        name="moments",
    )(in_hbm(dosage), observed, chosen)


def finish_moments(sums):
    centre = sums[0:1] / sums[2:3]
    spread_inverse = 1.0 / jnp.sqrt(sums[1:2] / sums[2:3] - centre * centre + EPSILON)
    return jnp.concatenate([centre, spread_inverse], axis=0)


def flags_in(facts_ref, block):
    start = pl.multiple_of(pl.program_id(0) * block, block)
    return mask_of(facts_ref[2:3, pl.ds(start, block)])


def standardize(values, present, moments):
    spread = (values.astype(jnp.float32) - moments[0:1]) * moments[1:2]
    return jnp.where(present, spread, 0.0).astype(jnp.bfloat16)


def decode(ref, facts_ref, present, first):
    parts = []
    for low in range(0, ref.shape[1], present.shape[1]):
        part = slice(low, low + present.shape[1])
        place = slice(first + low, first + low + present.shape[1])
        spread = ref[:, part].astype(jnp.float32) - facts_ref[0:1, place]
        spread = spread * facts_ref[1:2, place]
        parts.append(jnp.where(present, spread, 0.0).astype(jnp.bfloat16))
    return parts[0] if len(parts) == 1 else jnp.concatenate(parts, axis=1)


def cross(left, right):
    return lax.dot_general(
        left, right, (((0,), (0,)), ((), ())), preferred_element_type=jnp.float32
    )


def first_kernel(
    observed_ref,
    above_ref,
    below_ref,
    own_ref,
    above_f,
    below_f,
    out_ref,
    above_out,
    below_out,
):
    peers, _, edge = out_ref.shape
    rows = own_ref.shape[1] // peers
    kept = edge // peers

    @pl.when(pl.program_id(0) == 0)
    def _():
        out_ref[...] = jnp.zeros_like(out_ref)

    own_present = mask_of(observed_ref[...])
    block = above_ref.shape[0]
    above_present = flags_in(above_f, block)
    below_present = flags_in(below_f, block)
    above = decode(above_ref, above_f, above_present, 0)
    below = decode(below_ref, below_f, below_present, 0)
    above_out[...] = above
    below_out[...] = below
    near = cross(own_ref[...], above)
    far = cross(below, above)
    shares = [
        jnp.sum(jnp.where(other & above_present, 1.0, 0.0), axis=0, keepdims=True)
        for other in (own_present, below_present)
    ]
    for k in range(peers):
        out_ref[k, :rows, :] += near[k * rows : (k + 1) * rows]
        out_ref[k, rows : rows + kept, :] += far[k * kept : (k + 1) * kept]
        for low in range(0, edge, 128):
            out_ref[k, rows + kept : rows + kept + 1, low : low + 128] += shares[0]
            out_ref[k, rows + kept + 1 : rows + kept + 2, low : low + 128] += shares[1]


def first_pass(observed, above, below, own, above_f, below_f, peers):
    samples, width = own.shape
    edge = above.shape[1]
    block = block_of(samples)
    tall = (peers, width // peers + edge // peers + 8, edge)

    def rows_of(cut):
        return pl.BlockSpec((block, cut), lambda i: (i, 0))

    flags = pl.BlockSpec(above_f.shape, lambda i: (0, 0))
    flops = 2 * samples * edge * (width + edge)
    return pl.pallas_call(
        first_kernel,
        grid=(samples // block,),
        out_shape=(like(tall, jnp.float32),) + (like((samples, edge), jnp.bfloat16),) * 2,
        in_specs=[pl.BlockSpec((1, block), lambda i: (0, i))]
        + [rows_of(edge), rows_of(edge), rows_of(width), flags, flags],
        out_specs=(pl.BlockSpec(tall, lambda i: (0, 0, 0)), rows_of(edge), rows_of(edge)),
        compiler_params=pltpu.CompilerParams(vmem_limit_bytes=GRANT),
        cost_estimate=pl.CostEstimate(
            flops=flops, bytes_accessed=12 * samples * edge, transcendentals=0
        ),
        name="first",
    )(observed, above, below, own, above_f, below_f)


def second_kernel(
    above_ref,
    below_ref,
    above_1,
    below_1,
    own_ref,
    above_f,
    below_f,
    out_ref,
):
    peers, _, rest = out_ref.shape
    width, edge = own_ref.shape[1], above_1.shape[1]
    rows, kept, tail = width // peers, edge // peers, rest // peers

    @pl.when(pl.program_id(0) == 0)
    def _():
        out_ref[...] = jnp.zeros_like(out_ref)

    block = above_ref.shape[0]
    above = decode(above_ref, above_f, flags_in(above_f, block), edge)
    below = decode(below_ref, below_f, flags_in(below_f, block), edge)
    near = cross(own_ref[...], above)
    far = cross(below_1[...], above)
    last = cross(below, above_1[...])
    corner = cross(below, above)
    for k in range(peers):
        out_ref[k, :rows, :] += near[k * rows : (k + 1) * rows]
        low = rows + kept
        out_ref[k, rows:low, :] += far[k * kept : (k + 1) * kept]
        for left in range(0, edge, rest):
            out_ref[k, low : low + tail, :] += last[k * tail : (k + 1) * tail, left : left + rest]
            low += tail
        out_ref[k, low : low + tail, :] += corner[k * tail : (k + 1) * tail]


def second_pass(
    above, below, above_1, below_1, own, above_f, below_f, peers
):
    samples, width = own.shape
    edge, rest = above_1.shape[1], above.shape[1]
    block = block_of(samples)
    tall = (peers, (width + edge + width) // peers, rest)

    def rows_of(cut):
        return pl.BlockSpec((block, cut), lambda i: (i, 0))

    flags = pl.BlockSpec(above_f.shape, lambda i: (0, 0))
    flops = 2 * samples * rest * (2 * width + edge)
    return pl.pallas_call(
        second_kernel,
        grid=(samples // block,),
        out_shape=like(tall, jnp.float32),
        in_specs=[rows_of(rest)] * 2 + [rows_of(edge)] * 2 + [rows_of(width)] + [flags] * 2,
        out_specs=pl.BlockSpec(tall, lambda i: (0, 0, 0)),
        compiler_params=pltpu.CompilerParams(vmem_limit_bytes=GRANT),
        cost_estimate=pl.CostEstimate(
            flops=flops, bytes_accessed=2 * samples * (2 * width + edge), transcendentals=0
        ),
        name="second",
    )(above, below, above_1, below_1, own, above_f, below_f)


def per_device(dosage, observed, band_reach):
    samples, width = dosage.shape
    peers = lax.axis_size("samp")
    rows = width // peers
    kept = 3 * rows // 4
    tail = rows - kept
    edge, rest = kept * peers, tail * peers
    owners = np.arange(peers)[:, None] * rows
    order = np.concatenate(
        [
            (owners + np.arange(0, kept)[None, :]).ravel(),
            (owners + np.arange(kept, rows)[None, :]).ravel(),
        ]
    )
    pieces = width // rest
    chosen = (np.arange(width)[:, None] == order[None, :]).astype(jnp.bfloat16)
    up_1, down_1 = head_pass(dosage, jnp.asarray(order[None, :edge], jnp.int32))
    below_1 = from_below(up_1, "var")
    above_1 = from_above(down_1, "var")
    down_2, up_2, sums = moments_pass(dosage, observed, chosen[:, edge:])
    sums = sum_all(sums, "samp")
    moments = finish_moments(sums)
    cuts = [(k * rows, k * rows + kept) for k in range(peers)]
    cuts += [(k * rows + kept, (k + 1) * rows) for k in range(peers)]
    ordered = jnp.concatenate([moments[:, low:high] for low, high in cuts], axis=1)
    above_f, below_f = [
        jnp.concatenate(
            [jnp.pad(part, ((0, 0), (0, samples - width))), observed.astype(jnp.float32)]
        )
        for part in (moments, ordered)
    ]
    below_f = from_below(below_f, "var")
    above_f = from_above(above_f, "var")
    below_2 = from_below(up_2, "var")
    above_2 = from_above(down_2, "var")
    own = standardize(dosage, (observed[0] != 0)[:, None], moments)
    own = lax.optimization_barrier(own)
    same = sum_rows(cross(own, own).reshape(peers, rows, width), "samp")
    one, above_1, below_1 = first_pass(
        observed, above_1, below_1, own, above_f, below_f, peers
    )
    one = sum_rows(one, "samp")
    shares = jnp.maximum(one[rows + kept :], 1.0)
    near_1 = one[:rows] / shares[0:1]
    far_1 = one[rows : rows + kept] / shares[1:2]
    far_1 = from_above(far_1, "var")
    two = second_pass(
        above_2, below_2, above_1, below_1, own, above_f, below_f, peers
    )
    two = sum_rows(two, "samp")
    far_2 = two[rows:] / shares[1:2, :rest]
    far_2 = from_above(far_2, "var")
    near = jnp.concatenate([near_1, two[:rows] / shares[0:1, :rest]], axis=1)
    low = [far_2[kept + k * tail : kept + (k + 1) * tail] for k in range(pieces)]
    far = jnp.concatenate(
        [
            jnp.concatenate([far_1, far_2[:kept]], axis=1),
            jnp.concatenate(low, axis=1),
        ],
        axis=0,
    )
    result = jnp.stack([same / jnp.maximum(sums[2:3], 1.0), near, far], axis=1)
    keep = jnp.arange(BAND, dtype=jnp.int32) <= band_reach[0]
    return jnp.where(keep[None, :, None], result, jnp.float32(0.0))[None]


def solution(mesh):
    return jax.shard_map(
        per_device,
        mesh=mesh,
        in_specs=(P("samp", ("seg", "var")), P(("seg", "var"), "samp"), P(("seg", "var"))),
        out_specs=P(("seg", "var"), "samp", None, None),
        check_vma=False,
    )
```

```python
import functools

import jax
import jax.numpy as jnp
import numpy as np
from jax import lax
from jax.experimental import pallas as pl
from jax.experimental.pallas import tpu as pltpu
from jax.sharding import PartitionSpec as P

BAND = 3


EPSILON = 1e-05


def from_above(shard, axis):
    peers = lax.axis_size(axis)
    return lax.ppermute(shard, axis, [(i, i - 1) for i in range(1, peers)])


def from_below(shard, axis):
    peers = lax.axis_size(axis)
    return lax.ppermute(shard, axis, [(i, i + 1) for i in range(peers - 2)])


def swap(shard, axis, bit):
    peers = lax.axis_size(axis)
    return lax.ppermute(shard, axis, [(i, i ^ bit) for i in range(peers)])


def bits_of(peers):
    return [1 << k for k in range(peers.bit_length() - 1)]


def sum_all(value, axis):
    for bit in bits_of(lax.axis_size(axis)):
        value = value + swap(value, axis, bit)
    return value


def sum_rows(partial, axis, exact=None):
    place = lax.axis_index(axis)
    for bit in bits_of(lax.axis_size(axis)):
        pairs = partial.reshape(partial.shape[0] // 2, 2, *partial.shape[1:])
        high = (place & bit) != 0
        keep = jnp.where(high, pairs[:, 1], pairs[:, 0])
        give = jnp.where(high, pairs[:, 0], pairs[:, 1])
        if bit == 1 or exact is None:
            got = swap(give, axis, bit)
        else:
            rows = give.shape[1]
            near = lax.reduce_precision(give, 8, 7)
            left = (give[:, exact:] - near[:, exact:]).astype(jnp.bfloat16)
            got = jnp.concatenate([near.astype(jnp.bfloat16), left], axis=1)
            got = swap(got, axis, bit).astype(jnp.float32)
            left = got[:, rows:]
            got = got[:, :rows]
            if rows > exact:
                got = jnp.concatenate([got[:, :exact], got[:, exact:] + left], axis=1)
        partial = keep + got
    return partial[0]


GRANT = 20 << 20


def block_of(samples):
    return 512 if samples % 512 == 0 else samples


def in_hbm(array):
    return pltpu.with_memory_space_constraint(array, pltpu.HBM)


def like(shape, dtype):
    return jax.ShapeDtypeStruct(shape, dtype)


def mask_of(row):
    lanes = 128
    return jnp.transpose(jnp.broadcast_to(row.astype(jnp.float32), (lanes, row.shape[1]))) > 0.5


def head_kernel(kept, rows, dosage_ref, up_ref, down_ref, held, up_held, down_held, sems):
    samples, width = dosage_ref.shape
    edge = up_ref.shape[1]
    block = block_of(samples) // 2

    def move(source, target, kind, k):
        part = pl.ds(k * block, block)
        copy = pltpu.make_async_copy(source.at[part, :], target.at[part, :], sems.at[kind, k])
        copy.start()
        return copy

    arriving = [move(dosage_ref, held, 0, k) for k in range(samples // block)]
    leaving = []
    for k, copy in enumerate(arriving):
        part = pl.ds(k * block, block)
        copy.wait()
        values = held[part, :]
        owners = [values[:, low : low + kept] for low in range(0, width, rows)]
        up_held[part, :] = jnp.concatenate(owners, axis=1)
        leaving.append(move(up_held, up_ref, 1, k))
        down_held[part, :] = held[part, :edge]
        leaving.append(move(down_held, down_ref, 2, k))
    for copy in leaving:
        copy.wait()


def whole():
    return pl.BlockSpec(memory_space=pltpu.VMEM)


def head_pass(dosage, kept, rows):
    samples, width = dosage.shape
    edge = width // rows * kept
    half = jnp.bfloat16
    return pl.pallas_call(
        functools.partial(head_kernel, kept, rows),
        out_shape=(like((samples, edge), half),) * 2,
        in_specs=[pl.BlockSpec(memory_space=pl.ANY)],
        out_specs=(pl.BlockSpec(memory_space=pl.ANY),) * 2,
        scratch_shapes=[
            pltpu.VMEM((samples, width), half),
            pltpu.VMEM((samples, edge), half),
            pltpu.VMEM((samples, edge), half),
            pltpu.SemaphoreType.DMA((3, 2 * samples // block_of(samples))),
        ],
        compiler_params=pltpu.CompilerParams(vmem_limit_bytes=GRANT),
        name="head",
    )(in_hbm(dosage))


def moments_kernel(dosage_ref, observed_ref, chosen_ref, down_2, up_2, sums_ref):
    width = dosage_ref.shape[1]
    lanes = 128

    @pl.when(pl.program_id(0) == 0)
    def _():
        sums_ref[...] = jnp.zeros_like(sums_ref)

    present = mask_of(observed_ref[...])
    count = jnp.sum(jnp.where(present, 1.0, 0.0), axis=0, keepdims=True)
    for low in range(0, width, lanes):
        part = slice(low, low + lanes)
        kept = jnp.where(present, dosage_ref[:, part].astype(jnp.float32), 0.0)
        sums_ref[0:1, part] += jnp.sum(kept, axis=0, keepdims=True)
        sums_ref[1:2, part] += jnp.sum(kept * kept, axis=0, keepdims=True)
        sums_ref[2:3, part] += count
    down_2[...] = dosage_ref[:, width - down_2.shape[1] :]
    up = jnp.dot(dosage_ref[...], chosen_ref[...], preferred_element_type=jnp.float32)
    up_2[...] = up.astype(jnp.bfloat16)


def moments_pass(dosage, observed, chosen):
    samples, width = dosage.shape
    block, rest = block_of(samples), chosen.shape[1]
    return pl.pallas_call(
        moments_kernel,
        grid=(samples // block,),
        out_shape=(like((samples, rest), jnp.bfloat16),) * 2 + (like((8, width), jnp.float32),),
        in_specs=[
            pl.BlockSpec((block, width), lambda i: (i, 0)),
            pl.BlockSpec((1, block), lambda i: (0, i)),
            pl.BlockSpec((width, rest), lambda i: (0, 0)),
        ],
        out_specs=(pl.BlockSpec((block, rest), lambda i: (i, 0)),) * 2
        + (pl.BlockSpec((8, width), lambda i: (0, 0)),),
        compiler_params=pltpu.CompilerParams(vmem_limit_bytes=GRANT),
        cost_estimate=pl.CostEstimate(
            flops=2 * samples * width * rest,
            bytes_accessed=2 * samples * (width + 2 * rest),
            transcendentals=0,
        ),
        name="moments",
    )(in_hbm(dosage), observed, chosen)


def finish_moments(sums):
    centre = sums[0:1] / sums[2:3]
    spread_inverse = 1.0 / jnp.sqrt(sums[1:2] / sums[2:3] - centre * centre + EPSILON)
    return jnp.concatenate([centre, spread_inverse], axis=0)


def standardize(values, present, moments):
    spread = (values.astype(jnp.float32) - moments[0:1]) * moments[1:2]
    return jnp.where(present, spread, 0.0).astype(jnp.bfloat16)


def decode(values, facts_ref, present, first):
    parts = []
    for low in range(0, values.shape[1], present.shape[1]):
        part = slice(low, low + present.shape[1])
        place = slice(first + low, first + low + present.shape[1])
        spread = values[:, part].astype(jnp.float32) - facts_ref[0:1, place]
        spread = spread * facts_ref[1:2, place]
        parts.append(jnp.where(present, spread, 0.0).astype(jnp.bfloat16))
    return parts[0] if len(parts) == 1 else jnp.concatenate(parts, axis=1)


def cross(left, right):
    return lax.dot_general(
        left, right, (((0,), (0,)), ((), ())), preferred_element_type=jnp.float32
    )


def first_kernel(
    observed_ref,
    above_ref,
    below_ref,
    own_ref,
    above_f,
    below_f,
    out_ref,
    above_out,
    below_out,
    above_held,
    below_held,
    sems,
):
    peers, _, edge = out_ref.shape
    samples = own_ref.shape[0]
    rows = own_ref.shape[1] // peers
    kept = edge // peers
    block = block_of(samples)

    def move(source, target, kind, k):
        part = pl.ds(k * block, block)
        copy = pltpu.make_async_copy(source.at[part, :], target.at[part, :], sems.at[kind, k])
        copy.start()
        return copy

    arriving = []
    for k in range(samples // block):
        arriving.append(
            (move(above_ref, above_held, 0, k), move(below_ref, below_held, 1, k))
        )
    shares = [jnp.zeros((1, 128), jnp.float32)] * 2
    for k, copies in enumerate(arriving):
        part = slice(k * block, (k + 1) * block)
        own_present = mask_of(observed_ref[:, part])
        above_present = mask_of(above_f[2:3, part])
        below_present = mask_of(below_f[2:3, part])
        shares = [
            share
            + jnp.sum(jnp.where(other & above_present, 1.0, 0.0), axis=0, keepdims=True)
            for share, other in zip(shares, (own_present, below_present))
        ]
        copies[0].wait()
        above = decode(above_held[part, :], above_f, above_present, 0)
        above_out[part, :] = above
        near = cross(own_ref[part, :], above)
        copies[1].wait()
        below = decode(below_held[part, :], below_f, below_present, 0)
        below_out[part, :] = below
        far = cross(below, above)
        for owner in range(peers):
            into = out_ref.at[owner]
            add_to(into, slice(0, rows), near[owner * rows : (owner + 1) * rows], k)
            add_to(into, slice(rows, rows + kept), far[owner * kept : (owner + 1) * kept], k)
    for owner in range(peers):
        for low in range(0, edge, 128):
            out_ref[owner, rows + kept : rows + kept + 1, low : low + 128] = shares[0]
            out_ref[owner, rows + kept + 1 : rows + kept + 2, low : low + 128] = shares[1]
        out_ref[owner, rows + kept + 2 :, :] = jnp.zeros((6, edge), jnp.float32)


def add_to(ref, part, value, step):
    ref[part, :] = value if step == 0 else ref[part, :] + value


def first_pass(observed, above, below, own, above_f, below_f, peers):
    samples, width = own.shape
    edge = above.shape[1]
    half = jnp.bfloat16
    tall = (peers, width // peers + edge // peers + 8, edge)
    anywhere = pl.BlockSpec(memory_space=pl.ANY)
    return pl.pallas_call(
        first_kernel,
        out_shape=(like(tall, jnp.float32),) + (like((samples, edge), half),) * 2,
        in_specs=[whole(), anywhere, anywhere, whole(), whole(), whole()],
        out_specs=(whole(),) * 3,
        scratch_shapes=[
            pltpu.VMEM((samples, edge), half),
            pltpu.VMEM((samples, edge), half),
            pltpu.SemaphoreType.DMA((2, samples // block_of(samples))),
        ],
        compiler_params=pltpu.CompilerParams(vmem_limit_bytes=GRANT),
        cost_estimate=pl.CostEstimate(
            flops=2 * samples * edge * (width + edge),
            bytes_accessed=12 * samples * edge,
            transcendentals=0,
        ),
        name="first",
    )(observed, in_hbm(above), in_hbm(below), own, above_f, below_f)


def second_kernel(
    above_ref, below_ref, above_1, below_1, own_ref, above_f, below_f, out_ref
):
    peers, _, rest = out_ref.shape
    samples, width = own_ref.shape
    edge = above_1.shape[1]
    rows, kept, tail = width // peers, edge // peers, rest // peers
    block = block_of(samples)
    for k in range(samples // block):
        part = slice(k * block, (k + 1) * block)
        above = decode(above_ref[part, :], above_f, mask_of(above_f[2:3, part]), edge)
        below = decode(below_ref[part, :], below_f, mask_of(below_f[2:3, part]), edge)
        far = cross(below_1[part, :], above)
        last = cross(below, above_1[part, :])
        corner = cross(below, above)
        near = cross(own_ref[part, :], above)
        for owner in range(peers):
            into = out_ref.at[owner]
            add_to(into, slice(0, rows), near[owner * rows : (owner + 1) * rows], k)
            low = rows + kept
            add_to(into, slice(rows, low), far[owner * kept : (owner + 1) * kept], k)
            lines = slice(owner * tail, (owner + 1) * tail)
            for left in range(0, edge, rest):
                add_to(into, slice(low, low + tail), last[lines, left : left + rest], k)
                low += tail
            add_to(into, slice(low, low + tail), corner[lines], k)


def second_pass(above, below, above_1, below_1, own, above_f, below_f, peers):
    samples, width = own.shape
    edge, rest = above_1.shape[1], above.shape[1]
    tall = (peers, (width + edge + width) // peers, rest)
    return pl.pallas_call(
        second_kernel,
        out_shape=like(tall, jnp.float32),
        in_specs=[whole()] * 7,
        out_specs=whole(),
        compiler_params=pltpu.CompilerParams(vmem_limit_bytes=GRANT),
        cost_estimate=pl.CostEstimate(
            flops=2 * samples * rest * (2 * width + edge),
            bytes_accessed=2 * samples * (2 * width + edge),
            transcendentals=0,
        ),
        name="second",
    )(above, below, above_1, below_1, own, above_f, below_f)


def per_device(dosage, observed, band_reach):
    samples, width = dosage.shape
    peers = lax.axis_size("samp")
    rows = width // peers
    kept = 3 * rows // 4
    tail = rows - kept
    edge, rest = kept * peers, tail * peers
    owners = np.arange(peers)[:, None] * rows
    order = np.concatenate(
        [
            (owners + np.arange(0, kept)[None, :]).ravel(),
            (owners + np.arange(kept, rows)[None, :]).ravel(),
        ]
    )
    pieces = width // rest
    chosen = (np.arange(width)[:, None] == order[None, :]).astype(jnp.bfloat16)
    up_1, down_1 = head_pass(dosage, kept, rows)
    below_1 = from_below(up_1, "var")
    above_1 = from_above(down_1, "var")
    down_2, up_2, sums = moments_pass(dosage, observed, chosen[:, edge:])
    sums = sum_all(sums, "samp")
    moments = finish_moments(sums)
    cuts = [(k * rows, k * rows + kept) for k in range(peers)]
    cuts += [(k * rows + kept, (k + 1) * rows) for k in range(peers)]
    ordered = jnp.concatenate([moments[:, low:high] for low, high in cuts], axis=1)
    above_f, below_f = [
        jnp.concatenate(
            [jnp.pad(part, ((0, 0), (0, samples - width))), observed.astype(jnp.float32)]
        )
        for part in (moments, ordered)
    ]
    below_f = from_below(below_f, "var")
    above_f = from_above(above_f, "var")
    below_2 = from_below(up_2, "var")
    above_2 = from_above(down_2, "var")
    own = standardize(dosage, (observed[0] != 0)[:, None], moments)
    own = lax.optimization_barrier(own)
    same = sum_rows(cross(own, own).reshape(peers, rows, width), "samp")
    one, above_1, below_1 = first_pass(
        observed, above_1, below_1, own, above_f, below_f, peers
    )
    one = sum_rows(one, "samp", rows + kept)
    shares = jnp.maximum(one[rows + kept :], 1.0)
    near_1 = one[:rows] / shares[0:1]
    far_1 = one[rows : rows + kept] / shares[1:2]
    two = second_pass(
        above_2, below_2, above_1, below_1, own, above_f, below_f, peers
    )
    two = sum_rows(two, "samp", two.shape[1])
    far_2 = two[rows:] / shares[1:2, :rest]
    low = [far_2[kept + k * tail : kept + (k + 1) * tail] for k in range(pieces)]
    far = jnp.concatenate(
        [
            jnp.concatenate([far_1, far_2[:kept]], axis=1),
            jnp.concatenate(low, axis=1),
        ],
        axis=0,
    )
    far = from_above(far, "var")
    near = jnp.concatenate([near_1, two[:rows] / shares[0:1, :rest]], axis=1)
    result = jnp.stack([same / jnp.maximum(sums[2:3], 1.0), near, far], axis=1)
    keep = jnp.arange(BAND, dtype=jnp.int32) <= band_reach[0]
    return jnp.where(keep[None, :, None], result, jnp.float32(0.0))[None]


def solution(mesh):
    return jax.shard_map(
        per_device,
        mesh=mesh,
        in_specs=(P("samp", ("seg", "var")), P(("seg", "var"), "samp"), P(("seg", "var"))),
        out_specs=P(("seg", "var"), "samp", None, None),
        check_vma=False,
    )
```

```python
import functools

import jax
import jax.numpy as jnp
from jax import lax
from jax.experimental import pallas as pl
from jax.experimental.pallas import tpu as pltpu
from jax.sharding import PartitionSpec as P

BAND = 3


EPSILON = 1e-05


def trade(shard, axis, first):
    peers = lax.axis_size(axis)
    pairs = [(i, i + 1) for i in range(first, peers - 1, 2)]
    return lax.ppermute(shard, axis, pairs + [(high, low) for low, high in pairs])


def bring_back(shard, axis):
    peers = lax.axis_size(axis)
    return lax.ppermute(shard, axis, [(i, i - 1) for i in range(1, peers - 1)])


def is_even():
    return lax.axis_index("var") % 2 == 0


def either(even, one, two):
    return jnp.where(even, one, two), jnp.where(even, two, one)


def swap(shard, axis, bit):
    peers = lax.axis_size(axis)
    return lax.ppermute(shard, axis, [(i, i ^ bit) for i in range(peers)])


def bits_of(peers):
    return [1 << k for k in range(peers.bit_length() - 1)]


def sum_all(value, axis):
    for bit in bits_of(lax.axis_size(axis)):
        value = value + swap(value, axis, bit)
    return value


def sum_rows(partial, axis, exact=None):
    place = lax.axis_index(axis)
    for bit in bits_of(lax.axis_size(axis)):
        pairs = partial.reshape(partial.shape[0] // 2, 2, *partial.shape[1:])
        high = (place & bit) != 0
        keep = jnp.where(high, pairs[:, 1], pairs[:, 0])
        give = jnp.where(high, pairs[:, 0], pairs[:, 1])
        if bit == 1 or exact is None:
            got = swap(give, axis, bit)
        else:
            rows = give.shape[1]
            near = lax.reduce_precision(give, 8, 7)
            left = (give[:, exact:] - near[:, exact:]).astype(jnp.bfloat16)
            got = jnp.concatenate([near.astype(jnp.bfloat16), left], axis=1)
            got = swap(got, axis, bit).astype(jnp.float32)
            left = got[:, rows:]
            got = got[:, :rows]
            if rows > exact:
                got = jnp.concatenate([got[:, :exact], got[:, exact:] + left], axis=1)
        partial = keep + got
    return partial[0]


GRANT = 20 << 20


def block_of(samples):
    return 512 if samples % 512 == 0 else samples


def in_hbm(array):
    return pltpu.with_memory_space_constraint(array, pltpu.HBM)


def like(shape, dtype):
    return jax.ShapeDtypeStruct(shape, dtype)


def mask_of(row):
    lanes = 128
    return jnp.transpose(jnp.broadcast_to(row.astype(jnp.float32), (lanes, row.shape[1]))) > 0.5


def head_kernel(kept, rows, dosage_ref, a_ref, b_ref, held, a_held, b_held, sems):
    samples, width = dosage_ref.shape
    edge = a_ref.shape[1]
    block = block_of(samples) // 2
    even = is_even()

    def move(source, target, kind, k):
        part = pl.ds(k * block, block)
        copy = pltpu.make_async_copy(source.at[part, :], target.at[part, :], sems.at[kind, k])
        copy.start()
        return copy

    arriving = [move(dosage_ref, held, 0, k) for k in range(samples // block)]
    leaving = []
    for k, copy in enumerate(arriving):
        part = pl.ds(k * block, block)
        copy.wait()
        values = held[part, :]
        owners = [values[:, low : low + kept] for low in range(0, width, rows)]
        up = jnp.concatenate(owners, axis=1)
        a_held[part, :], b_held[part, :] = either(even, up, values[:, :edge])
        leaving.append(move(a_held, a_ref, 1, k))
        leaving.append(move(b_held, b_ref, 2, k))
    for copy in leaving:
        copy.wait()


def whole():
    return pl.BlockSpec(memory_space=pltpu.VMEM)


def head_pass(dosage, kept, rows):
    samples, width = dosage.shape
    edge = width // rows * kept
    half = jnp.bfloat16
    return pl.pallas_call(
        functools.partial(head_kernel, kept, rows),
        out_shape=(like((samples, edge), half),) * 2,
        in_specs=[pl.BlockSpec(memory_space=pl.ANY)],
        out_specs=(pl.BlockSpec(memory_space=pl.ANY),) * 2,
        scratch_shapes=[
            pltpu.VMEM((samples, width), half),
            pltpu.VMEM((samples, edge), half),
            pltpu.VMEM((samples, edge), half),
            pltpu.SemaphoreType.DMA((3, 2 * samples // block_of(samples))),
        ],
        compiler_params=pltpu.CompilerParams(vmem_limit_bytes=GRANT),
        name="head",
    )(in_hbm(dosage))


def moments_kernel(kept, rows, dosage_ref, observed_ref, a_ref, b_ref, sums_ref):
    width = dosage_ref.shape[1]
    lanes = 128

    @pl.when(pl.program_id(0) == 0)
    def _():
        sums_ref[...] = jnp.zeros_like(sums_ref)

    present = mask_of(observed_ref[...])
    count = jnp.sum(jnp.where(present, 1.0, 0.0), axis=0, keepdims=True)
    for low in range(0, width, lanes):
        part = slice(low, low + lanes)
        seen = jnp.where(present, dosage_ref[:, part].astype(jnp.float32), 0.0)
        sums_ref[0:1, part] += jnp.sum(seen, axis=0, keepdims=True)
        sums_ref[1:2, part] += jnp.sum(seen * seen, axis=0, keepdims=True)
        sums_ref[2:3, part] += count
    values = dosage_ref[...]
    up = jnp.concatenate([values[:, low + kept : low + rows] for low in range(0, width, rows)], 1)
    down = values[:, width - a_ref.shape[1] :]
    a_ref[...], b_ref[...] = either(is_even(), up, down)


def moments_pass(dosage, observed, kept, rows):
    samples, width = dosage.shape
    block, rest = block_of(samples), width // rows * (rows - kept)
    return pl.pallas_call(
        functools.partial(moments_kernel, kept, rows),
        grid=(samples // block,),
        out_shape=(like((samples, rest), jnp.bfloat16),) * 2 + (like((8, width), jnp.float32),),
        in_specs=[
            pl.BlockSpec((block, width), lambda i: (i, 0)),
            pl.BlockSpec((1, block), lambda i: (0, i)),
        ],
        out_specs=(pl.BlockSpec((block, rest), lambda i: (i, 0)),) * 2
        + (pl.BlockSpec((8, width), lambda i: (0, 0)),),
        compiler_params=pltpu.CompilerParams(vmem_limit_bytes=GRANT),
        cost_estimate=pl.CostEstimate(
            flops=2 * samples * width * rest,
            bytes_accessed=2 * samples * (width + 2 * rest),
            transcendentals=0,
        ),
        name="moments",
    )(in_hbm(dosage), observed)


def facts_kernel(kept, rows, sums_ref, observed_ref, moments_ref, a_ref, b_ref):
    width = sums_ref.shape[1]
    totals = sums_ref[2:3, :]
    centre = sums_ref[0:1, :] / totals
    inverse = 1.0 / jnp.sqrt(sums_ref[1:2, :] / totals - centre * centre + EPSILON)
    moments_ref[0:1, :] = centre
    moments_ref[1:2, :] = inverse
    flags = observed_ref[...].astype(jnp.float32)
    even = is_even()
    cuts = [(low, low + kept) for low in range(0, width, rows)]
    cuts += [(low + kept, low + rows) for low in range(0, width, rows)]
    for line, natural in enumerate((centre, inverse)):
        ordered = jnp.concatenate([natural[:, low:high] for low, high in cuts], axis=1)
        one, two = either(even, ordered, natural)
        a_ref[line : line + 1, :width] = one
        b_ref[line : line + 1, :width] = two
    for ref in (a_ref, b_ref):
        ref[2:3, :] = flags
        if width < ref.shape[1]:
            ref[0:2, width:] = jnp.zeros((2, ref.shape[1] - width), jnp.float32)


def facts_pass(sums, observed, kept, rows):
    samples, width = observed.shape[1], sums.shape[1]
    single = jnp.float32
    return pl.pallas_call(
        functools.partial(facts_kernel, kept, rows),
        out_shape=(like((2, width), single),) + (like((3, samples), single),) * 2,
        in_specs=[whole()] * 2,
        out_specs=(whole(),) * 3,
        compiler_params=pltpu.CompilerParams(vmem_limit_bytes=GRANT),
        name="facts",
    )(sums, observed)


def standardize(values, present, moments):
    spread = (values.astype(jnp.float32) - moments[0:1]) * moments[1:2]
    return jnp.where(present, spread, 0.0).astype(jnp.bfloat16)


def decode(values, facts, present, first):
    parts = []
    for low in range(0, values.shape[1], present.shape[1]):
        part = slice(low, low + present.shape[1])
        place = slice(first + low, first + low + present.shape[1])
        spread = values[:, part].astype(jnp.float32) - facts[0:1, place]
        spread = spread * facts[1:2, place]
        parts.append(jnp.where(present, spread, 0.0).astype(jnp.bfloat16))
    return parts[0] if len(parts) == 1 else jnp.concatenate(parts, axis=1)


def cross(left, right):
    return lax.dot_general(
        left, right, (((0,), (0,)), ((), ())), preferred_element_type=jnp.float32
    )


def first_kernel(
    observed_ref,
    a_ref,
    b_ref,
    own_ref,
    a_facts,
    b_facts,
    out_ref,
    above_out,
    below_out,
    a_held,
    b_held,
    sems,
):
    peers, _, edge = out_ref.shape
    samples = own_ref.shape[0]
    rows = own_ref.shape[1] // peers
    kept = edge // peers
    block = block_of(samples)

    def move(source, target, kind, k):
        part = pl.ds(k * block, block)
        copy = pltpu.make_async_copy(source.at[part, :], target.at[part, :], sems.at[kind, k])
        copy.start()
        return copy

    arriving = []
    for k in range(samples // block):
        arriving.append(
            (move(a_ref, a_held, 0, k), move(b_ref, b_held, 1, k))
        )
    even = is_even()
    above_f, below_f = either(even, a_facts[...], b_facts[...])
    shares = [jnp.zeros((1, 128), jnp.float32)] * 2
    for k, copies in enumerate(arriving):
        part = slice(k * block, (k + 1) * block)
        own_present = mask_of(observed_ref[:, part])
        above_present = mask_of(above_f[2:3, part])
        below_present = mask_of(below_f[2:3, part])
        shares = [
            share
            + jnp.sum(jnp.where(other & above_present, 1.0, 0.0), axis=0, keepdims=True)
            for share, other in zip(shares, (own_present, below_present))
        ]
        copies[0].wait()
        copies[1].wait()
        above, below = either(even, a_held[part, :], b_held[part, :])
        above = decode(above, above_f, above_present, 0)
        above_out[part, :] = above
        near = cross(own_ref[part, :], above)
        below = decode(below, below_f, below_present, 0)
        below_out[part, :] = below
        far = cross(below, above)
        for owner in range(peers):
            into = out_ref.at[owner]
            add_to(into, slice(0, rows), near[owner * rows : (owner + 1) * rows], k)
            add_to(into, slice(rows, rows + kept), far[owner * kept : (owner + 1) * kept], k)
    for owner in range(peers):
        for low in range(0, edge, 128):
            out_ref[owner, rows + kept : rows + kept + 1, low : low + 128] = shares[0]
            out_ref[owner, rows + kept + 1 : rows + kept + 2, low : low + 128] = shares[1]
        out_ref[owner, rows + kept + 2 :, :] = jnp.zeros((6, edge), jnp.float32)


def add_to(ref, part, value, step):
    ref[part, :] = value if step == 0 else ref[part, :] + value


def first_pass(observed, above, below, own, above_f, below_f, peers):
    samples, width = own.shape
    edge = above.shape[1]
    half = jnp.bfloat16
    tall = (peers, width // peers + edge // peers + 8, edge)
    anywhere = pl.BlockSpec(memory_space=pl.ANY)
    return pl.pallas_call(
        first_kernel,
        out_shape=(like(tall, jnp.float32),) + (like((samples, edge), half),) * 2,
        in_specs=[whole(), anywhere, anywhere, whole(), whole(), whole()],
        out_specs=(whole(),) * 3,
        scratch_shapes=[
            pltpu.VMEM((samples, edge), half),
            pltpu.VMEM((samples, edge), half),
            pltpu.SemaphoreType.DMA((2, samples // block_of(samples))),
        ],
        compiler_params=pltpu.CompilerParams(vmem_limit_bytes=GRANT),
        cost_estimate=pl.CostEstimate(
            flops=2 * samples * edge * (width + edge),
            bytes_accessed=12 * samples * edge,
            transcendentals=0,
        ),
        name="first",
    )(observed, in_hbm(above), in_hbm(below), own, above_f, below_f)


def second_kernel(a_ref, b_ref, above_1, below_1, own_ref, a_facts, b_facts, out_ref):
    peers, _, rest = out_ref.shape
    samples, width = own_ref.shape
    edge = above_1.shape[1]
    rows, kept, tail = width // peers, edge // peers, rest // peers
    block = block_of(samples)
    even = is_even()
    above_f, below_f = either(even, a_facts[...], b_facts[...])
    for k in range(samples // block):
        part = slice(k * block, (k + 1) * block)
        above, below = either(even, a_ref[part, :], b_ref[part, :])
        above = decode(above, above_f, mask_of(above_f[2:3, part]), edge)
        below = decode(below, below_f, mask_of(below_f[2:3, part]), edge)
        far = cross(below_1[part, :], above)
        last = cross(below, above_1[part, :])
        corner = cross(below, above)
        near = cross(own_ref[part, :], above)
        for owner in range(peers):
            into = out_ref.at[owner]
            add_to(into, slice(0, rows), near[owner * rows : (owner + 1) * rows], k)
            low = rows + kept
            add_to(into, slice(rows, low), far[owner * kept : (owner + 1) * kept], k)
            lines = slice(owner * tail, (owner + 1) * tail)
            for left in range(0, edge, rest):
                add_to(into, slice(low, low + tail), last[lines, left : left + rest], k)
                low += tail
            add_to(into, slice(low, low + tail), corner[lines], k)


def second_pass(above, below, above_1, below_1, own, above_f, below_f, peers):
    samples, width = own.shape
    edge, rest = above_1.shape[1], above.shape[1]
    tall = (peers, (width + edge + width) // peers, rest)
    return pl.pallas_call(
        second_kernel,
        out_shape=like(tall, jnp.float32),
        in_specs=[whole()] * 7,
        out_specs=whole(),
        compiler_params=pltpu.CompilerParams(vmem_limit_bytes=GRANT),
        cost_estimate=pl.CostEstimate(
            flops=2 * samples * rest * (2 * width + edge),
            bytes_accessed=2 * samples * (2 * width + edge),
            transcendentals=0,
        ),
        name="second",
    )(above, below, above_1, below_1, own, above_f, below_f)


def per_device(dosage, observed, band_reach):
    _, width = dosage.shape
    peers = lax.axis_size("samp")
    rows = width // peers
    kept = 3 * rows // 4
    tail = rows - kept
    rest = tail * peers
    pieces = width // rest
    a_1, b_1 = head_pass(dosage, kept, rows)
    a_1 = trade(a_1, "var", 0)
    b_1 = trade(b_1, "var", 1)
    a_2, b_2, sums = moments_pass(dosage, observed, kept, rows)
    sums = sum_all(sums, "samp")
    moments, a_f, b_f = facts_pass(sums, observed, kept, rows)
    a_f = trade(a_f, "var", 0)
    b_f = trade(b_f, "var", 1)
    a_2 = trade(a_2, "var", 0)
    b_2 = trade(b_2, "var", 1)
    own = standardize(dosage, (observed[0] != 0)[:, None], moments)
    own = lax.optimization_barrier(own)
    same = sum_rows(cross(own, own).reshape(peers, rows, width), "samp")
    one, above_1, below_1 = first_pass(observed, a_1, b_1, own, a_f, b_f, peers)
    one = sum_rows(one, "samp", rows + kept)
    shares = jnp.maximum(one[rows + kept :], 1.0)
    near_1 = one[:rows] / shares[0:1]
    far_1 = one[rows : rows + kept] / shares[1:2]
    far_1 = bring_back(far_1, "var")
    two = second_pass(a_2, b_2, above_1, below_1, own, a_f, b_f, peers)
    two = sum_rows(two, "samp", two.shape[1])
    far_2 = two[rows:] / shares[1:2, :rest]
    far_2 = bring_back(far_2, "var")
    near = jnp.concatenate([near_1, two[:rows] / shares[0:1, :rest]], axis=1)
    low = [far_2[kept + k * tail : kept + (k + 1) * tail] for k in range(pieces)]
    far = jnp.concatenate(
        [
            jnp.concatenate([far_1, far_2[:kept]], axis=1),
            jnp.concatenate(low, axis=1),
        ],
        axis=0,
    )
    result = jnp.stack([same / jnp.maximum(sums[2:3], 1.0), near, far], axis=1)
    keep = jnp.arange(BAND, dtype=jnp.int32) <= band_reach[0]
    return jnp.where(keep[None, :, None], result, jnp.float32(0.0))[None]


def solution(mesh):
    return jax.shard_map(
        per_device,
        mesh=mesh,
        in_specs=(P("samp", ("seg", "var")), P(("seg", "var"), "samp"), P(("seg", "var"))),
        out_specs=P(("seg", "var"), "samp", None, None),
        check_vma=False,
    )
```

```python
import functools

import jax
import jax.numpy as jnp
from jax import lax
from jax.experimental import pallas as pl
from jax.experimental.pallas import tpu as pltpu
from jax.sharding import PartitionSpec as P

BAND = 3


EPSILON = 1e-05


def trade(shard, axis, first):
    peers = lax.axis_size(axis)
    pairs = [(i, i + 1) for i in range(first, peers - 1, 2)]
    return lax.ppermute(shard, axis, pairs + [(high, low) for low, high in pairs])


def bring_back(shard, axis):
    peers = lax.axis_size(axis)
    return lax.ppermute(shard, axis, [(i, i - 1) for i in range(1, peers - 1)])


def is_even():
    return lax.axis_index("var") % 2 == 0


def either(even, one, two):
    return jnp.where(even, one, two), jnp.where(even, two, one)


def swap(shard, axis, bit):
    peers = lax.axis_size(axis)
    return lax.ppermute(shard, axis, [(i, i ^ bit) for i in range(peers)])


def bits_of(peers):
    return [1 << k for k in range(peers.bit_length() - 1)]


def sum_all(value, axis):
    for bit in bits_of(lax.axis_size(axis)):
        value = value + swap(value, axis, bit)
    return value


def sum_rows(partial, axis, exact=None):
    place = lax.axis_index(axis)
    for bit in bits_of(lax.axis_size(axis)):
        pairs = partial.reshape(partial.shape[0] // 2, 2, *partial.shape[1:])
        high = (place & bit) != 0
        keep = jnp.where(high, pairs[:, 1], pairs[:, 0])
        give = jnp.where(high, pairs[:, 0], pairs[:, 1])
        if bit == 1 or exact is None:
            got = swap(give, axis, bit)
        else:
            rows = give.shape[1]
            near = lax.reduce_precision(give, 8, 7)
            left = (give[:, exact:] - near[:, exact:]).astype(jnp.bfloat16)
            got = jnp.concatenate([near.astype(jnp.bfloat16), left], axis=1)
            got = swap(got, axis, bit).astype(jnp.float32)
            left = got[:, rows:]
            got = got[:, :rows]
            if rows > exact:
                got = jnp.concatenate([got[:, :exact], got[:, exact:] + left], axis=1)
        partial = keep + got
    return partial[0]


GRANT = 20 << 20


def block_of(samples):
    return 512 if samples % 512 == 0 else samples


def in_hbm(array):
    return pltpu.with_memory_space_constraint(array, pltpu.HBM)


def like(shape, dtype):
    return jax.ShapeDtypeStruct(shape, dtype)


def mask_of(row):
    lanes = 128
    return jnp.transpose(jnp.broadcast_to(row.astype(jnp.float32), (lanes, row.shape[1]))) > 0.5


def head_kernel(kept, rows, dosage_ref, a_ref, b_ref, held, a_held, b_held, sems):
    samples, width = dosage_ref.shape
    edge = a_ref.shape[1]
    block = block_of(samples) // 2
    even = is_even()

    def move(source, target, kind, k):
        part = pl.ds(k * block, block)
        copy = pltpu.make_async_copy(source.at[part, :], target.at[part, :], sems.at[kind, k])
        copy.start()
        return copy

    arriving = [move(dosage_ref, held, 0, k) for k in range(samples // block)]
    leaving = []
    for k, copy in enumerate(arriving):
        part = pl.ds(k * block, block)
        copy.wait()
        values = held[part, :]
        owners = [values[:, low : low + kept] for low in range(0, width, rows)]
        up = jnp.concatenate(owners, axis=1)
        a_held[part, :], b_held[part, :] = either(even, up, values[:, :edge])
        leaving.append(move(a_held, a_ref, 1, k))
        leaving.append(move(b_held, b_ref, 2, k))
    for copy in leaving:
        copy.wait()


def whole():
    return pl.BlockSpec(memory_space=pltpu.VMEM)


def head_pass(dosage, kept, rows):
    samples, width = dosage.shape
    edge = width // rows * kept
    half = jnp.bfloat16
    return pl.pallas_call(
        functools.partial(head_kernel, kept, rows),
        out_shape=(like((samples, edge), half),) * 2,
        in_specs=[pl.BlockSpec(memory_space=pl.ANY)],
        out_specs=(pl.BlockSpec(memory_space=pl.ANY),) * 2,
        scratch_shapes=[
            pltpu.VMEM((samples, width), half),
            pltpu.VMEM((samples, edge), half),
            pltpu.VMEM((samples, edge), half),
            pltpu.SemaphoreType.DMA((3, 2 * samples // block_of(samples))),
        ],
        compiler_params=pltpu.CompilerParams(vmem_limit_bytes=GRANT),
        name="head",
    )(in_hbm(dosage))


def moments_kernel(kept, rows, dosage_ref, observed_ref, a_ref, b_ref, sums_ref):
    width = dosage_ref.shape[1]
    lanes = 128

    @pl.when(pl.program_id(0) == 0)
    def _():
        sums_ref[...] = jnp.zeros_like(sums_ref)

    present = mask_of(observed_ref[...])
    count = jnp.sum(jnp.where(present, 1.0, 0.0), axis=0, keepdims=True)
    for low in range(0, width, lanes):
        part = slice(low, low + lanes)
        seen = jnp.where(present, dosage_ref[:, part].astype(jnp.float32), 0.0)
        sums_ref[0:1, part] += jnp.sum(seen, axis=0, keepdims=True)
        sums_ref[1:2, part] += jnp.sum(seen * seen, axis=0, keepdims=True)
        sums_ref[2:3, part] += count
    values = dosage_ref[...]
    up = jnp.concatenate([values[:, low + kept : low + rows] for low in range(0, width, rows)], 1)
    down = values[:, width - a_ref.shape[1] :]
    a_ref[...], b_ref[...] = either(is_even(), up, down)


def moments_pass(dosage, observed, kept, rows):
    samples, width = dosage.shape
    block, rest = block_of(samples), width // rows * (rows - kept)
    return pl.pallas_call(
        functools.partial(moments_kernel, kept, rows),
        grid=(samples // block,),
        out_shape=(like((samples, rest), jnp.bfloat16),) * 2 + (like((8, width), jnp.float32),),
        in_specs=[
            pl.BlockSpec((block, width), lambda i: (i, 0)),
            pl.BlockSpec((1, block), lambda i: (0, i)),
        ],
        out_specs=(pl.BlockSpec((block, rest), lambda i: (i, 0)),) * 2
        + (pl.BlockSpec((8, width), lambda i: (0, 0)),),
        compiler_params=pltpu.CompilerParams(vmem_limit_bytes=GRANT),
        cost_estimate=pl.CostEstimate(
            flops=2 * samples * width * rest,
            bytes_accessed=2 * samples * (width + 2 * rest),
            transcendentals=0,
        ),
        name="moments",
    )(in_hbm(dosage), observed)


def facts_kernel(kept, rows, sums_ref, observed_ref, moments_ref, a_ref, b_ref):
    width = sums_ref.shape[1]
    totals = sums_ref[2:3, :]
    centre = sums_ref[0:1, :] / totals
    inverse = 1.0 / jnp.sqrt(sums_ref[1:2, :] / totals - centre * centre + EPSILON)
    moments_ref[0:1, :] = centre
    moments_ref[1:2, :] = inverse
    flags = observed_ref[...].astype(jnp.float32)
    even = is_even()
    cuts = [(low, low + kept) for low in range(0, width, rows)]
    cuts += [(low + kept, low + rows) for low in range(0, width, rows)]
    for line, natural in enumerate((centre, inverse)):
        ordered = jnp.concatenate([natural[:, low:high] for low, high in cuts], axis=1)
        one, two = either(even, ordered, natural)
        a_ref[line : line + 1, :width] = one
        b_ref[line : line + 1, :width] = two
    for ref in (a_ref, b_ref):
        ref[2:3, :] = flags
        if width < ref.shape[1]:
            ref[0:2, width:] = jnp.zeros((2, ref.shape[1] - width), jnp.float32)


def facts_pass(sums, observed, kept, rows):
    samples, width = observed.shape[1], sums.shape[1]
    single = jnp.float32
    return pl.pallas_call(
        functools.partial(facts_kernel, kept, rows),
        out_shape=(like((2, width), single),) + (like((3, samples), single),) * 2,
        in_specs=[whole()] * 2,
        out_specs=(whole(),) * 3,
        compiler_params=pltpu.CompilerParams(vmem_limit_bytes=GRANT),
        name="facts",
    )(sums, observed)


def standardize(values, present, moments):
    spread = (values.astype(jnp.float32) - moments[0:1]) * moments[1:2]
    return jnp.where(present, spread, 0.0).astype(jnp.bfloat16)


def decode(values, facts, present, first):
    parts = []
    for low in range(0, values.shape[1], present.shape[1]):
        part = slice(low, low + present.shape[1])
        place = slice(first + low, first + low + present.shape[1])
        spread = values[:, part].astype(jnp.float32) - facts[0:1, place]
        spread = spread * facts[1:2, place]
        parts.append(jnp.where(present, spread, 0.0).astype(jnp.bfloat16))
    return parts[0] if len(parts) == 1 else jnp.concatenate(parts, axis=1)


def cross(left, right):
    return lax.dot_general(
        left, right, (((0,), (0,)), ((), ())), preferred_element_type=jnp.float32
    )


def first_kernel(
    observed_ref,
    a_ref,
    b_ref,
    own_ref,
    a_facts,
    b_facts,
    out_ref,
    above_out,
    below_out,
    a_held,
    b_held,
    sems,
):
    peers, _, edge = out_ref.shape
    samples = own_ref.shape[0]
    rows = own_ref.shape[1] // peers
    kept = edge // peers
    block = block_of(samples)

    def move(source, target, kind, k):
        part = pl.ds(k * block, block)
        copy = pltpu.make_async_copy(source.at[part, :], target.at[part, :], sems.at[kind, k])
        copy.start()
        return copy

    arriving = []
    for k in range(samples // block):
        arriving.append(
            (move(a_ref, a_held, 0, k), move(b_ref, b_held, 1, k))
        )
    even = is_even()
    above_f, below_f = either(even, a_facts[...], b_facts[...])
    shares = [jnp.zeros((1, 128), jnp.float32)] * 2
    for k, copies in enumerate(arriving):
        part = slice(k * block, (k + 1) * block)
        own_present = mask_of(observed_ref[:, part])
        above_present = mask_of(above_f[2:3, part])
        below_present = mask_of(below_f[2:3, part])
        shares = [
            share
            + jnp.sum(jnp.where(other & above_present, 1.0, 0.0), axis=0, keepdims=True)
            for share, other in zip(shares, (own_present, below_present))
        ]
        copies[0].wait()
        copies[1].wait()
        above, below = either(even, a_held[part, :], b_held[part, :])
        above = decode(above, above_f, above_present, 0)
        above_out[part, :] = above
        near = cross(own_ref[part, :], above)
        below = decode(below, below_f, below_present, 0)
        below_out[part, :] = below
        far = cross(below, above)
        for owner in range(peers):
            into = out_ref.at[owner]
            add_to(into, slice(0, rows), near[owner * rows : (owner + 1) * rows], k)
            add_to(into, slice(rows, rows + kept), far[owner * kept : (owner + 1) * kept], k)
    for owner in range(peers):
        for low in range(0, edge, 128):
            out_ref[owner, rows + kept : rows + kept + 1, low : low + 128] = shares[0]
            out_ref[owner, rows + kept + 1 : rows + kept + 2, low : low + 128] = shares[1]
        out_ref[owner, rows + kept + 2 :, :] = jnp.zeros((6, edge), jnp.float32)


def add_to(ref, part, value, step):
    ref[part, :] = value if step == 0 else ref[part, :] + value


def first_pass(observed, above, below, own, above_f, below_f, peers):
    samples, width = own.shape
    edge = above.shape[1]
    half = jnp.bfloat16
    tall = (peers, width // peers + edge // peers + 8, edge)
    anywhere = pl.BlockSpec(memory_space=pl.ANY)
    return pl.pallas_call(
        first_kernel,
        out_shape=(like(tall, jnp.float32),) + (like((samples, edge), half),) * 2,
        in_specs=[whole(), anywhere, anywhere, whole(), whole(), whole()],
        out_specs=(whole(),) * 3,
        scratch_shapes=[
            pltpu.VMEM((samples, edge), half),
            pltpu.VMEM((samples, edge), half),
            pltpu.SemaphoreType.DMA((2, samples // block_of(samples))),
        ],
        compiler_params=pltpu.CompilerParams(vmem_limit_bytes=GRANT),
        cost_estimate=pl.CostEstimate(
            flops=2 * samples * edge * (width + edge),
            bytes_accessed=12 * samples * edge,
            transcendentals=0,
        ),
        name="first",
    )(observed, in_hbm(above), in_hbm(below), own, above_f, below_f)


def second_kernel(a_ref, b_ref, above_1, below_1, a_facts, b_facts, out_ref, above_out):
    peers, _, rest = out_ref.shape
    samples, edge = above_1.shape
    kept, tail = edge // peers, rest // peers
    block = block_of(samples)
    even = is_even()
    above_f, below_f = either(even, a_facts[...], b_facts[...])
    for k in range(samples // block):
        part = slice(k * block, (k + 1) * block)
        above, below = either(even, a_ref[part, :], b_ref[part, :])
        above = decode(above, above_f, mask_of(above_f[2:3, part]), edge)
        below = decode(below, below_f, mask_of(below_f[2:3, part]), edge)
        above_out[part, :] = above
        far = cross(below_1[part, :], above)
        last = cross(below, above_1[part, :])
        corner = cross(below, above)
        for owner in range(peers):
            into = out_ref.at[owner]
            low = kept
            add_to(into, slice(0, low), far[owner * kept : (owner + 1) * kept], k)
            lines = slice(owner * tail, (owner + 1) * tail)
            for left in range(0, edge, rest):
                add_to(into, slice(low, low + tail), last[lines, left : left + rest], k)
                low += tail
            add_to(into, slice(low, low + tail), corner[lines], k)


def second_pass(a_2, b_2, above_1, below_1, a_facts, b_facts, peers):
    samples, edge = above_1.shape
    rest = a_2.shape[1]
    tall = (peers, (edge + edge + rest) // peers, rest)
    return pl.pallas_call(
        second_kernel,
        out_shape=(like(tall, jnp.float32), like((samples, rest), jnp.bfloat16)),
        in_specs=[whole()] * 6,
        out_specs=(whole(),) * 2,
        compiler_params=pltpu.CompilerParams(vmem_limit_bytes=GRANT),
        cost_estimate=pl.CostEstimate(
            flops=2 * samples * rest * (2 * edge + rest),
            bytes_accessed=4 * samples * (edge + rest),
            transcendentals=0,
        ),
        name="second",
    )(a_2, b_2, above_1, below_1, a_facts, b_facts)


def per_device(dosage, observed, band_reach):
    _, width = dosage.shape
    peers = lax.axis_size("samp")
    rows = width // peers
    kept = 3 * rows // 4
    tail = rows - kept
    rest = tail * peers
    pieces = width // rest
    a_1, b_1 = head_pass(dosage, kept, rows)
    a_1 = trade(a_1, "var", 0)
    b_1 = trade(b_1, "var", 1)
    a_2, b_2, sums = moments_pass(dosage, observed, kept, rows)
    sums = sum_all(sums, "samp")
    moments, a_f, b_f = facts_pass(sums, observed, kept, rows)
    a_f = trade(a_f, "var", 0)
    b_f = trade(b_f, "var", 1)
    a_2 = trade(a_2, "var", 0)
    b_2 = trade(b_2, "var", 1)
    own = standardize(dosage, (observed[0] != 0)[:, None], moments)
    own = lax.optimization_barrier(own)
    same = sum_rows(cross(own, own).reshape(peers, rows, width), "samp")
    one, above_1, below_1 = first_pass(observed, a_1, b_1, own, a_f, b_f, peers)
    one = sum_rows(one, "samp", rows + kept)
    shares = jnp.maximum(one[rows + kept :], 1.0)
    near_1 = one[:rows] / shares[0:1]
    far_1 = one[rows : rows + kept] / shares[1:2]
    far_1 = bring_back(far_1, "var")
    two, above_2 = second_pass(a_2, b_2, above_1, below_1, a_f, b_f, peers)
    far_2 = sum_rows(two, "samp", two.shape[1]) / shares[1:2, :rest]
    far_2 = bring_back(far_2, "var")
    near_2 = cross(own, above_2).reshape(peers, rows, rest)
    near_2 = sum_rows(near_2, "samp", rows) / shares[0:1, :rest]
    near = jnp.concatenate([near_1, near_2], axis=1)
    same = same / jnp.maximum(sums[2:3], 1.0)
    low = [far_2[kept + k * tail : kept + (k + 1) * tail] for k in range(pieces)]
    far = jnp.concatenate(
        [
            jnp.concatenate([far_1, far_2[:kept]], axis=1),
            jnp.concatenate(low, axis=1),
        ],
        axis=0,
    )
    planes = [same, near] + [jnp.zeros_like(same)] * (BAND - 2)
    planes = [
        jnp.where(k <= band_reach[0], plane, 0.0) for k, plane in enumerate(planes)
    ]
    result = lax.optimization_barrier(jnp.stack(planes, axis=0))
    far = jnp.where(BAND - 1 <= band_reach[0], far, 0.0)
    result = lax.dynamic_update_index_in_dim(result, far, BAND - 1, 0)
    return jnp.transpose(result, (1, 0, 2))[None]


def solution(mesh):
    return jax.shard_map(
        per_device,
        mesh=mesh,
        in_specs=(P("samp", ("seg", "var")), P(("seg", "var"), "samp"), P(("seg", "var"))),
        out_specs=P(("seg", "var"), "samp", None, None),
        check_vma=False,
    )
```

```python
import functools

import jax
import jax.numpy as jnp
from jax import lax
from jax.experimental import pallas as pl
from jax.experimental.pallas import tpu as pltpu
from jax.sharding import PartitionSpec as P

BAND = 3


EPSILON = 1e-05


def trade(shard, axis, first):
    peers = lax.axis_size(axis)
    pairs = [(i, i + 1) for i in range(first, peers - 1, 2)]
    return lax.ppermute(shard, axis, pairs + [(high, low) for low, high in pairs])


def bring_back(shard, axis):
    peers = lax.axis_size(axis)
    return lax.ppermute(shard, axis, [(i, i - 1) for i in range(1, peers - 1)])


def is_even():
    return lax.axis_index("var") % 2 == 0


def either(even, one, two):
    return jnp.where(even, one, two), jnp.where(even, two, one)


def swap(shard, axis, bit):
    peers = lax.axis_size(axis)
    return lax.ppermute(shard, axis, [(i, i ^ bit) for i in range(peers)])


def bits_of(peers):
    return [1 << k for k in range(peers.bit_length() - 1)]


def sum_all(value, axis):
    for bit in bits_of(lax.axis_size(axis)):
        value = value + swap(value, axis, bit)
    return value


def sum_rows(partial, axis, roles, exact=None):
    for bit in bits_of(lax.axis_size(axis)):
        pairs = partial.reshape(partial.shape[0] // 2, 2, *partial.shape[1:])
        keep = jnp.where(roles[bit], pairs[:, 1], pairs[:, 0])
        give = jnp.where(roles[bit], pairs[:, 0], pairs[:, 1])
        if bit == 1 or exact is None:
            got = swap(give, axis, bit)
        else:
            rows = give.shape[1]
            near = lax.reduce_precision(give, 8, 7)
            left = (give[:, exact:] - near[:, exact:]).astype(jnp.bfloat16)
            got = jnp.concatenate([near.astype(jnp.bfloat16), left], axis=1)
            got = swap(got, axis, bit).astype(jnp.float32)
            left = got[:, rows:]
            got = got[:, :rows]
            if rows > exact:
                got = jnp.concatenate([got[:, :exact], got[:, exact:] + left], axis=1)
        partial = keep + got
    return partial[0]


GRANT = 20 << 20


def block_of(samples):
    return 512 if samples % 512 == 0 else samples


def in_hbm(array):
    return pltpu.with_memory_space_constraint(array, pltpu.HBM)


def like(shape, dtype):
    return jax.ShapeDtypeStruct(shape, dtype)


def mask_of(row):
    lanes = 128
    return jnp.transpose(jnp.broadcast_to(row.astype(jnp.float32), (lanes, row.shape[1]))) > 0.5


def head_kernel(kept, rows, dosage_ref, a_ref, b_ref, held, sems):
    samples, width = dosage_ref.shape
    edge = a_ref.shape[1]
    block = block_of(samples) // 2
    even = is_even()
    copies = []
    for k in range(samples // block):
        part = pl.ds(k * block, block)
        copy = pltpu.make_async_copy(dosage_ref.at[part, :], held.at[part, :], sems.at[k])
        copy.start()
        copies.append(copy)
    for k, copy in enumerate(copies):
        part = pl.ds(k * block, block)
        copy.wait()
        values = held[part, :]
        owners = [values[:, low : low + kept] for low in range(0, width, rows)]
        up = jnp.concatenate(owners, axis=1)
        a_ref[part, :], b_ref[part, :] = either(even, up, values[:, :edge])


def whole():
    return pl.BlockSpec(memory_space=pltpu.VMEM)


def head_pass(dosage, kept, rows):
    samples, width = dosage.shape
    edge = width // rows * kept
    half = jnp.bfloat16
    return pl.pallas_call(
        functools.partial(head_kernel, kept, rows),
        out_shape=(like((samples, edge), half),) * 2,
        in_specs=[pl.BlockSpec(memory_space=pl.ANY)],
        out_specs=(whole(),) * 2,
        scratch_shapes=[
            pltpu.VMEM((samples, width), half),
            pltpu.SemaphoreType.DMA((2 * samples // block_of(samples),)),
        ],
        compiler_params=pltpu.CompilerParams(vmem_limit_bytes=GRANT),
        name="head",
    )(in_hbm(dosage))


def moments_kernel(cuts, rows, dosage_ref, observed_ref, *refs):
    width = dosage_ref.shape[1]
    lanes = 128
    peers = width // rows
    sums_ref = refs[-1]

    @pl.when(pl.program_id(0) == 0)
    def _():
        sums_ref[...] = jnp.zeros_like(sums_ref)

    present = mask_of(observed_ref[...])
    count = jnp.sum(jnp.where(present, 1.0, 0.0), axis=0, keepdims=True)
    for low in range(0, width, lanes):
        part = slice(low, low + lanes)
        seen = jnp.where(present, dosage_ref[:, part].astype(jnp.float32), 0.0)
        sums_ref[0:1, part] += jnp.sum(seen, axis=0, keepdims=True)
        sums_ref[1:2, part] += jnp.sum(seen * seen, axis=0, keepdims=True)
        sums_ref[2:3, part] += count
    values = dosage_ref[...]
    for k, (low, high) in enumerate(cuts):
        owners = [values[:, first + low : first + high] for first in range(0, width, rows)]
        up = jnp.concatenate(owners, axis=1)
        down = values[:, low * peers : high * peers]
        refs[2 * k][...], refs[2 * k + 1][...] = either(is_even(), up, down)


def moments_pass(dosage, observed, cuts, rows):
    samples, width = dosage.shape
    block = block_of(samples)
    sizes = [(high - low) * width // rows for low, high in cuts for _ in range(2)]
    return pl.pallas_call(
        functools.partial(moments_kernel, cuts, rows),
        grid=(samples // block,),
        out_shape=tuple(like((samples, size), jnp.bfloat16) for size in sizes)
        + (like((8, width), jnp.float32),),
        in_specs=[
            pl.BlockSpec((block, width), lambda i: (i, 0)),
            pl.BlockSpec((1, block), lambda i: (0, i)),
        ],
        out_specs=tuple(pl.BlockSpec((block, size), lambda i: (i, 0)) for size in sizes)
        + (pl.BlockSpec((8, width), lambda i: (0, 0)),),
        compiler_params=pltpu.CompilerParams(vmem_limit_bytes=GRANT),
        cost_estimate=pl.CostEstimate(
            flops=8 * samples * width, bytes_accessed=4 * samples * width, transcendentals=0
        ),
        name="moments",
    )(in_hbm(dosage), observed)


def facts_kernel(cuts, rows, sums_ref, observed_ref, moments_ref, a_ref, b_ref):
    width = sums_ref.shape[1]
    totals = sums_ref[2:3, :]
    centre = sums_ref[0:1, :] / totals
    inverse = 1.0 / jnp.sqrt(sums_ref[1:2, :] / totals - centre * centre + EPSILON)
    moments_ref[0:1, :] = centre
    moments_ref[1:2, :] = inverse
    flags = observed_ref[...].astype(jnp.float32)
    even = is_even()
    cuts = [(first + low, first + high) for low, high in cuts for first in range(0, width, rows)]
    for line, natural in enumerate((centre, inverse)):
        ordered = jnp.concatenate([natural[:, low:high] for low, high in cuts], axis=1)
        one, two = either(even, ordered, natural)
        a_ref[line : line + 1, :width] = one
        b_ref[line : line + 1, :width] = two
    for ref in (a_ref, b_ref):
        ref[2:3, :] = flags
        if width < ref.shape[1]:
            ref[0:2, width:] = jnp.zeros((2, ref.shape[1] - width), jnp.float32)


def facts_pass(sums, observed, cuts, rows):
    samples, width = observed.shape[1], sums.shape[1]
    single = jnp.float32
    return pl.pallas_call(
        functools.partial(facts_kernel, cuts, rows),
        out_shape=(like((2, width), single),) + (like((3, samples), single),) * 2,
        in_specs=[whole()] * 2,
        out_specs=(whole(),) * 3,
        compiler_params=pltpu.CompilerParams(vmem_limit_bytes=GRANT),
        name="facts",
    )(sums, observed)


def standardize(values, present, moments):
    spread = (values.astype(jnp.float32) - moments[0:1]) * moments[1:2]
    return jnp.where(present, spread, 0.0).astype(jnp.bfloat16)


def decode(values, facts, present, first):
    parts = []
    for low in range(0, values.shape[1], present.shape[1]):
        part = slice(low, low + present.shape[1])
        place = slice(first + low, first + low + present.shape[1])
        spread = values[:, part].astype(jnp.float32) - facts[0:1, place]
        spread = spread * facts[1:2, place]
        parts.append(jnp.where(present, spread, 0.0).astype(jnp.bfloat16))
    return parts[0] if len(parts) == 1 else jnp.concatenate(parts, axis=1)


def cross(left, right):
    return lax.dot_general(
        left, right, (((0,), (0,)), ((), ())), preferred_element_type=jnp.float32
    )


def chunk_kernel(step, marks, last, observed_ref, a_ref, b_ref, a_facts, b_facts, *refs):
    lanes = 128
    olds = refs[: 2 * min(step, 1)]
    out_ref, *fresh_refs = refs[len(olds) :]
    peers = out_ref.shape[0]
    samples, _ = a_ref.shape
    old = olds[0].shape[1] if olds else 0
    block = block_of(samples)
    even = is_even()
    above_f, below_f = either(even, a_facts[...], b_facts[...])
    shares = [jnp.zeros((1, lanes), jnp.float32)] * 2
    for k in range(samples // block):
        part = slice(k * block, (k + 1) * block)
        above_present = mask_of(above_f[2:3, part])
        below_present = mask_of(below_f[2:3, part])
        if step == 0:
            own_present = mask_of(observed_ref[:, part])
            shares = [
                share
                + jnp.sum(jnp.where(other & above_present, 1.0, 0.0), axis=0, keepdims=True)
                for share, other in zip(shares, (own_present, below_present))
            ]
        above, below = either(even, a_ref[part, :], b_ref[part, :])
        above = decode(above, above_f, above_present, old)
        below = decode(below, below_f, below_present, old)
        if last:
            fresh_refs[0][part, :] = above
        else:
            for ref, value, earlier in zip(fresh_refs, (above, below), olds or (None, None)):
                if old:
                    ref[part, :old] = earlier[part, :]
                ref[part, old:] = value
        products = []
        if old:
            product = cross(olds[1][part, :], above)
            for low, high in zip(marks[:step], marks[1 : step + 1]):
                products.append(product[low * peers : high * peers])
            products.append(cross(below, olds[0][part, :]))
        products.append(cross(below, above))
        for owner in range(peers):
            into = out_ref.at[owner]
            low = 0
            for product in products:
                tall = product.shape[0] // peers
                for left in range(0, product.shape[1], lanes):
                    value = product[owner * tall : (owner + 1) * tall, left : left + lanes]
                    add_to(into, slice(low, low + tall), value, k)
                    low += tall
    if step == 0:
        low = out_ref.shape[1] - 8
        for owner in range(peers):
            out_ref[owner, low : low + 1, :] = shares[0]
            out_ref[owner, low + 1 : low + 2, :] = shares[1]
            out_ref[owner, low + 2 :, :] = jnp.zeros((6, lanes), jnp.float32)


def add_to(ref, part, value, step):
    ref[part, :] = value if step == 0 else ref[part, :] + value


def chunk_pass(step, marks, peers, observed, a, b, a_facts, b_facts, olds):
    samples, fresh = a.shape
    last = step == len(marks) - 2
    lanes = 128
    old = olds[0].shape[1] if olds else 0
    lines = (2 * old * fresh + fresh * fresh) // (peers * lanes) + (8 if step == 0 else 0)
    stored = like((samples, fresh if last else old + fresh), jnp.bfloat16)
    results = (like((peers, lines, lanes), jnp.float32),) + (stored,) * (1 if last else 2)
    return pl.pallas_call(
        functools.partial(chunk_kernel, step, marks, last),
        out_shape=results,
        in_specs=[whole()] * (5 + len(olds)),
        out_specs=(whole(),) * len(results),
        compiler_params=pltpu.CompilerParams(vmem_limit_bytes=GRANT),
        cost_estimate=pl.CostEstimate(
            flops=2 * samples * lines * peers * lanes,
            bytes_accessed=8 * samples * fresh,
            transcendentals=0,
        ),
    )(observed, a, b, a_facts, b_facts, *olds)


def unpack(lines, shapes):
    blocks, low = [], 0
    for tall, wide in shapes:
        pieces = []
        for _ in range(wide // lines.shape[1]):
            pieces.append(lines[low : low + tall])
            low += tall
        blocks.append(jnp.concatenate(pieces, axis=1) if len(pieces) > 1 else pieces[0])
    return blocks


def per_device(dosage, observed, band_reach):
    _, width = dosage.shape
    peers = lax.axis_size("samp")
    rows = width // peers
    marks = (0, rows // 2, 3 * rows // 4, rows)
    cuts = tuple(zip(marks[:-1], marks[1:]))
    heights = [high - low for low, high in cuts]
    wides = [height * peers for height in heights]
    a_1, b_1 = head_pass(dosage, heights[0], rows)
    a_1 = trade(a_1, "var", 0)
    b_1 = trade(b_1, "var", 1)
    place = lax.axis_index("samp")
    roles = {bit: (place & bit) != 0 for bit in bits_of(peers)}
    a_2, b_2, a_3, b_3, sums = moments_pass(dosage, observed, cuts[1:], rows)
    sums = sum_all(sums, "samp")
    moments, a_f, b_f = facts_pass(sums, observed, cuts, rows)
    a_f = trade(a_f, "var", 0)
    b_f = trade(b_f, "var", 1)
    a_2 = trade(a_2, "var", 0)
    b_2 = trade(b_2, "var", 1)
    a_3 = trade(a_3, "var", 0)
    b_3 = trade(b_3, "var", 1)
    own = standardize(dosage, (observed[0] != 0)[:, None], moments)
    own = lax.optimization_barrier(own)
    same = sum_rows(cross(own, own).reshape(peers, rows, width), "samp", roles)
    chunks = [(a_1, b_1), (a_2, b_2), (a_3, b_3)]
    products, olds, aboves = [], [], []
    for step, (a, b) in enumerate(chunks):
        product, *olds = chunk_pass(step, marks, peers, observed, a, b, a_f, b_f, olds)
        products.append(product)
        aboves.append(olds[0])
    shapes = [
        [(heights[j], wides[step]) for j in range(step)]
        + [(heights[step], wides[j]) for j in range(step + 1)]
        for step in range(3)
    ]
    lines = products[1].shape[1] + products[0].shape[1] - 8
    one = jnp.concatenate([products[1], products[0]], axis=1)
    one = sum_rows(one, "samp", roles, lines)
    shares = jnp.maximum(one[lines:], 1.0)
    far_1 = one[:lines] / shares[1:2]
    far_1 = bring_back(far_1, "var")
    near_1 = cross(own, aboves[1]).reshape(peers, rows, -1)
    near_1 = sum_rows(near_1, "samp", roles, rows)
    near_1 = near_1 / jnp.concatenate([shares[0:1]] * (near_1.shape[1] // 128), axis=1)
    far_2 = sum_rows(products[2], "samp", roles, products[2].shape[1]) / shares[1:2]
    far_2 = bring_back(far_2, "var")
    near_2 = cross(own, aboves[2]).reshape(peers, rows, -1)
    near_2 = sum_rows(near_2, "samp", roles, rows) / shares[0:1]
    early = unpack(far_1, shapes[1] + shapes[0])
    near = jnp.concatenate([near_1, near_2], axis=1)
    same = same / jnp.maximum(sums[2:3], 1.0)
    late = unpack(far_2, shapes[2])
    far = jnp.concatenate(
        [
            jnp.concatenate([early[3], early[0], late[0]], axis=1),
            jnp.concatenate([early[1], early[2], late[1]], axis=1),
            jnp.concatenate(late[2:], axis=1),
        ],
        axis=0,
    )
    planes = [same, near] + [jnp.zeros_like(same)] * (BAND - 2)
    planes = [
        jnp.where(k <= band_reach[0], plane, 0.0) for k, plane in enumerate(planes)
    ]
    result = lax.optimization_barrier(jnp.stack(planes, axis=0))
    far = jnp.where(BAND - 1 <= band_reach[0], far, 0.0)
    result = lax.dynamic_update_index_in_dim(result, far, BAND - 1, 0)
    return jnp.transpose(result, (1, 0, 2))[None]


def solution(mesh):
    return jax.shard_map(
        per_device,
        mesh=mesh,
        in_specs=(P("samp", ("seg", "var")), P(("seg", "var"), "samp"), P(("seg", "var"))),
        out_specs=P(("seg", "var"), "samp", None, None),
        check_vma=False,
    )
```

```python
import functools

import jax
import jax.numpy as jnp
from jax import lax
from jax.experimental import pallas as pl
from jax.experimental.pallas import tpu as pltpu
from jax.sharding import PartitionSpec as P

BAND = 3


EPSILON = 1e-05


def trade(shard, axis, first):
    peers = lax.axis_size(axis)
    pairs = [(i, i + 1) for i in range(first, peers - 1, 2)]
    return lax.ppermute(shard, axis, pairs + [(high, low) for low, high in pairs])


def bring_back(shard, axis):
    peers = lax.axis_size(axis)
    return lax.ppermute(shard, axis, [(i, i - 1) for i in range(1, peers - 1)])


def is_even():
    return lax.axis_index("var") % 2 == 0


def either(even, one, two):
    return jnp.where(even, one, two), jnp.where(even, two, one)


def swap(shard, axis, bit):
    peers = lax.axis_size(axis)
    return lax.ppermute(shard, axis, [(i, i ^ bit) for i in range(peers)])


def bits_of(peers):
    return [1 << k for k in range(peers.bit_length() - 1)]


def sum_all(value, axis):
    for bit in bits_of(lax.axis_size(axis)):
        value = value + swap(value, axis, bit)
    return value


def sum_rows(partial, axis, roles, exact=None):
    for bit in bits_of(lax.axis_size(axis)):
        pairs = partial.reshape(partial.shape[0] // 2, 2, *partial.shape[1:])
        keep = jnp.where(roles[bit], pairs[:, 1], pairs[:, 0])
        give = jnp.where(roles[bit], pairs[:, 0], pairs[:, 1])
        if bit == 1 or exact is None:
            got = swap(give, axis, bit)
        else:
            rows = give.shape[1]
            near = lax.reduce_precision(give, 8, 7)
            left = (give[:, exact:] - near[:, exact:]).astype(jnp.bfloat16)
            got = jnp.concatenate([near.astype(jnp.bfloat16), left], axis=1)
            got = swap(got, axis, bit).astype(jnp.float32)
            left = got[:, rows:]
            got = got[:, :rows]
            if rows > exact:
                got = jnp.concatenate([got[:, :exact], got[:, exact:] + left], axis=1)
        partial = keep + got
    return partial[0]


GRANT = 20 << 20


def block_of(samples):
    return 512 if samples % 512 == 0 else samples


def in_hbm(array):
    return pltpu.with_memory_space_constraint(array, pltpu.HBM)


def like(shape, dtype):
    return jax.ShapeDtypeStruct(shape, dtype)


def mask_of(row):
    lanes = 128
    return jnp.transpose(jnp.broadcast_to(row.astype(jnp.float32), (lanes, row.shape[1]))) > 0.5


def head_kernel(kept, rows, dosage_ref, a_ref, b_ref, held, sems):
    samples, width = dosage_ref.shape
    edge = a_ref.shape[1]
    block = block_of(samples) // 2
    even = is_even()
    copies = []
    for k in range(samples // block):
        part = pl.ds(k * block, block)
        copy = pltpu.make_async_copy(dosage_ref.at[part, :], held.at[part, :], sems.at[k])
        copy.start()
        copies.append(copy)
    for k, copy in enumerate(copies):
        part = pl.ds(k * block, block)
        copy.wait()
        values = held[part, :]
        owners = [values[:, low : low + kept] for low in range(0, width, rows)]
        up = jnp.concatenate(owners, axis=1)
        a_ref[part, :], b_ref[part, :] = either(even, up, values[:, :edge])


def whole():
    return pl.BlockSpec(memory_space=pltpu.VMEM)


def head_pass(dosage, kept, rows):
    samples, width = dosage.shape
    edge = width // rows * kept
    half = jnp.bfloat16
    return pl.pallas_call(
        functools.partial(head_kernel, kept, rows),
        out_shape=(like((samples, edge), half),) * 2,
        in_specs=[pl.BlockSpec(memory_space=pl.ANY)],
        out_specs=(whole(),) * 2,
        scratch_shapes=[
            pltpu.VMEM((samples, width), half),
            pltpu.SemaphoreType.DMA((2 * samples // block_of(samples),)),
        ],
        compiler_params=pltpu.CompilerParams(vmem_limit_bytes=GRANT),
        name="head",
    )(in_hbm(dosage))


def moments_kernel(cuts, rows, dosage_ref, observed_ref, *refs):
    width = dosage_ref.shape[1]
    lanes = 128
    peers = width // rows
    sums_ref = refs[-1]

    @pl.when(pl.program_id(0) == 0)
    def _():
        sums_ref[...] = jnp.zeros_like(sums_ref)

    present = mask_of(observed_ref[...])
    count = jnp.sum(jnp.where(present, 1.0, 0.0), axis=0, keepdims=True)
    for low in range(0, width, lanes):
        part = slice(low, low + lanes)
        seen = jnp.where(present, dosage_ref[:, part].astype(jnp.float32), 0.0)
        sums_ref[0:1, part] += jnp.sum(seen, axis=0, keepdims=True)
        sums_ref[1:2, part] += jnp.sum(seen * seen, axis=0, keepdims=True)
        sums_ref[2:3, part] += count
    values = dosage_ref[...]
    for k, (low, high) in enumerate(cuts):
        owners = [values[:, first + low : first + high] for first in range(0, width, rows)]
        up = jnp.concatenate(owners, axis=1)
        down = values[:, low * peers : high * peers]
        refs[2 * k][...], refs[2 * k + 1][...] = either(is_even(), up, down)


def moments_pass(dosage, observed, cuts, rows):
    samples, width = dosage.shape
    block = block_of(samples)
    sizes = [(high - low) * width // rows for low, high in cuts for _ in range(2)]
    return pl.pallas_call(
        functools.partial(moments_kernel, cuts, rows),
        grid=(samples // block,),
        out_shape=tuple(like((samples, size), jnp.bfloat16) for size in sizes)
        + (like((8, width), jnp.float32),),
        in_specs=[
            pl.BlockSpec((block, width), lambda i: (i, 0)),
            pl.BlockSpec((1, block), lambda i: (0, i)),
        ],
        out_specs=tuple(pl.BlockSpec((block, size), lambda i: (i, 0)) for size in sizes)
        + (pl.BlockSpec((8, width), lambda i: (0, 0)),),
        compiler_params=pltpu.CompilerParams(vmem_limit_bytes=GRANT),
        cost_estimate=pl.CostEstimate(
            flops=8 * samples * width, bytes_accessed=4 * samples * width, transcendentals=0
        ),
        name="moments",
    )(in_hbm(dosage), observed)


def facts_kernel(cuts, rows, sums_ref, observed_ref, moments_ref, a_ref, b_ref):
    width = sums_ref.shape[1]
    totals = sums_ref[2:3, :]
    centre = sums_ref[0:1, :] / totals
    inverse = 1.0 / jnp.sqrt(sums_ref[1:2, :] / totals - centre * centre + EPSILON)
    moments_ref[0:1, :] = centre
    moments_ref[1:2, :] = inverse
    flags = observed_ref[...].astype(jnp.float32)
    even = is_even()
    cuts = [(first + low, first + high) for low, high in cuts for first in range(0, width, rows)]
    for line, natural in enumerate((centre, inverse)):
        ordered = jnp.concatenate([natural[:, low:high] for low, high in cuts], axis=1)
        one, two = either(even, ordered, natural)
        a_ref[line : line + 1, :width] = one
        b_ref[line : line + 1, :width] = two
    for ref in (a_ref, b_ref):
        ref[2:3, :] = flags
        if width < ref.shape[1]:
            ref[0:2, width:] = jnp.zeros((2, ref.shape[1] - width), jnp.float32)


def facts_pass(sums, observed, cuts, rows):
    samples, width = observed.shape[1], sums.shape[1]
    single = jnp.float32
    return pl.pallas_call(
        functools.partial(facts_kernel, cuts, rows),
        out_shape=(like((2, width), single),) + (like((3, samples), single),) * 2,
        in_specs=[whole()] * 2,
        out_specs=(whole(),) * 3,
        compiler_params=pltpu.CompilerParams(vmem_limit_bytes=GRANT),
        name="facts",
    )(sums, observed)


def standardize(values, present, moments):
    spread = (values.astype(jnp.float32) - moments[0:1]) * moments[1:2]
    return jnp.where(present, spread, 0.0).astype(jnp.bfloat16)


def decode(values, facts, present, first):
    parts = []
    for low in range(0, values.shape[1], present.shape[1]):
        part = slice(low, low + present.shape[1])
        place = slice(first + low, first + low + present.shape[1])
        spread = values[:, part].astype(jnp.float32) - facts[0:1, place]
        spread = spread * facts[1:2, place]
        parts.append(jnp.where(present, spread, 0.0).astype(jnp.bfloat16))
    return parts[0] if len(parts) == 1 else jnp.concatenate(parts, axis=1)


def cross(left, right):
    return lax.dot_general(
        left, right, (((0,), (0,)), ((), ())), preferred_element_type=jnp.float32
    )


def chunk_kernel(step, marks, last, observed_ref, a_ref, b_ref, a_facts, b_facts, *refs):
    lanes = 128
    olds = refs[: 2 * min(step, 1)]
    out_ref, *fresh_refs = refs[len(olds) :]
    peers = out_ref.shape[0]
    samples, _ = a_ref.shape
    old = olds[0].shape[1] if olds else 0
    block = block_of(samples)
    even = is_even()
    above_f, below_f = either(even, a_facts[...], b_facts[...])
    shares = [jnp.zeros((1, lanes), jnp.float32)] * 2
    for k in range(samples // block):
        part = slice(k * block, (k + 1) * block)
        above_present = mask_of(above_f[2:3, part])
        below_present = mask_of(below_f[2:3, part])
        if step == 0:
            own_present = mask_of(observed_ref[:, part])
            shares = [
                share
                + jnp.sum(jnp.where(other & above_present, 1.0, 0.0), axis=0, keepdims=True)
                for share, other in zip(shares, (own_present, below_present))
            ]
        above, below = either(even, a_ref[part, :], b_ref[part, :])
        above = decode(above, above_f, above_present, old)
        below = decode(below, below_f, below_present, old)
        if last:
            fresh_refs[0][part, :] = above
        else:
            for ref, value, earlier in zip(fresh_refs, (above, below), olds or (None, None)):
                if old:
                    ref[part, :old] = earlier[part, :]
                ref[part, old:] = value
        products = []
        if old:
            product = cross(olds[1][part, :], above)
            for low, high in zip(marks[:step], marks[1 : step + 1]):
                products.append(product[low * peers : high * peers])
            products.append(cross(below, olds[0][part, :]))
        products.append(cross(below, above))
        for owner in range(peers):
            into = out_ref.at[owner]
            low = 0
            for product in products:
                tall = product.shape[0] // peers
                for left in range(0, product.shape[1], lanes):
                    value = product[owner * tall : (owner + 1) * tall, left : left + lanes]
                    add_to(into, slice(low, low + tall), value, k)
                    low += tall
    if step == 0:
        low = out_ref.shape[1] - 8
        for owner in range(peers):
            out_ref[owner, low : low + 1, :] = shares[0]
            out_ref[owner, low + 1 : low + 2, :] = shares[1]
            out_ref[owner, low + 2 :, :] = jnp.zeros((6, lanes), jnp.float32)


def add_to(ref, part, value, step):
    ref[part, :] = value if step == 0 else ref[part, :] + value


def chunk_pass(step, marks, peers, observed, a, b, a_facts, b_facts, olds):
    samples, fresh = a.shape
    last = step == len(marks) - 2
    lanes = 128
    old = olds[0].shape[1] if olds else 0
    lines = (2 * old * fresh + fresh * fresh) // (peers * lanes) + (8 if step == 0 else 0)
    stored = like((samples, fresh if last else old + fresh), jnp.bfloat16)
    results = (like((peers, lines, lanes), jnp.float32),) + (stored,) * (1 if last else 2)
    return pl.pallas_call(
        functools.partial(chunk_kernel, step, marks, last),
        out_shape=results,
        in_specs=[whole()] * (5 + len(olds)),
        out_specs=(whole(),) * len(results),
        compiler_params=pltpu.CompilerParams(vmem_limit_bytes=GRANT),
        cost_estimate=pl.CostEstimate(
            flops=2 * samples * lines * peers * lanes,
            bytes_accessed=8 * samples * fresh,
            transcendentals=0,
        ),
    )(observed, a, b, a_facts, b_facts, *olds)


def unpack(lines, shapes):
    blocks, low = [], 0
    for tall, wide in shapes:
        pieces = []
        for _ in range(wide // lines.shape[1]):
            pieces.append(lines[low : low + tall])
            low += tall
        blocks.append(jnp.concatenate(pieces, axis=1) if len(pieces) > 1 else pieces[0])
    return blocks


def per_device(dosage, observed, band_reach):
    _, width = dosage.shape
    peers = lax.axis_size("samp")
    rows = width // peers
    marks = (0, rows // 2, 3 * rows // 4, rows)
    cuts = tuple(zip(marks[:-1], marks[1:]))
    heights = [high - low for low, high in cuts]
    wides = [height * peers for height in heights]
    a_1, b_1 = head_pass(dosage, heights[0], rows)
    a_1 = trade(a_1, "var", 0)
    b_1 = trade(b_1, "var", 1)
    place = lax.axis_index("samp")
    roles = {bit: (place & bit) != 0 for bit in bits_of(peers)}
    a_2, b_2, a_3, b_3, sums = moments_pass(dosage, observed, cuts[1:], rows)
    sums = sum_all(sums, "samp")
    moments, a_f, b_f = facts_pass(sums, observed, cuts, rows)
    a_f = trade(a_f, "var", 0)
    b_f = trade(b_f, "var", 1)
    a_2 = trade(a_2, "var", 0)
    b_2 = trade(b_2, "var", 1)
    a_3 = trade(a_3, "var", 0)
    b_3 = trade(b_3, "var", 1)
    own = standardize(dosage, (observed[0] != 0)[:, None], moments)
    own = lax.optimization_barrier(own)
    same = sum_rows(cross(own, own).reshape(peers, rows, width), "samp", roles)
    chunks = [(a_1, b_1), (a_2, b_2), (a_3, b_3)]
    products, olds, aboves = [], [], []
    for step, (a, b) in enumerate(chunks):
        product, *olds = chunk_pass(step, marks, peers, observed, a, b, a_f, b_f, olds)
        products.append(product)
        aboves.append(olds[0])
    shapes = [
        [(heights[j], wides[step]) for j in range(step)]
        + [(heights[step], wides[j]) for j in range(step + 1)]
        for step in range(3)
    ]
    lines = products[1].shape[1] + products[0].shape[1] - 8
    one = jnp.concatenate([products[1], products[0]], axis=1)
    one = sum_rows(one, "samp", roles, lines)
    shares = jnp.maximum(one[lines:], 1.0)
    far_1 = one[:lines] / shares[1:2]
    far_1 = bring_back(far_1, "var")
    near_1 = cross(own, aboves[1]).reshape(peers, rows, -1)
    near_1 = sum_rows(near_1, "samp", roles, rows)
    near_1 = near_1 / jnp.concatenate([shares[0:1]] * (near_1.shape[1] // 128), axis=1)
    far_2 = sum_rows(products[2], "samp", roles, products[2].shape[1]) / shares[1:2]
    far_2 = bring_back(far_2, "var")
    near_2 = cross(own, aboves[2]).reshape(peers, rows, -1)
    near_2 = sum_rows(near_2, "samp", roles, rows) / shares[0:1]
    early = unpack(far_1, shapes[1] + shapes[0])
    near = jnp.concatenate([near_1, near_2], axis=1)
    same = same / jnp.maximum(sums[2:3], 1.0)
    late = unpack(far_2, shapes[2])
    far = jnp.concatenate(
        [
            jnp.concatenate([early[3], early[0], late[0]], axis=1),
            jnp.concatenate([early[1], early[2], late[1]], axis=1),
            jnp.concatenate(late[2:], axis=1),
        ],
        axis=0,
    )
    result = jnp.stack([same, near, far], axis=1)
    keep = jnp.arange(BAND, dtype=jnp.int32) <= band_reach[0]
    return jnp.where(keep[None, :, None], result, jnp.float32(0.0))[None]


def solution(mesh):
    return jax.shard_map(
        per_device,
        mesh=mesh,
        in_specs=(P("samp", ("seg", "var")), P(("seg", "var"), "samp"), P(("seg", "var"))),
        out_specs=P(("seg", "var"), "samp", None, None),
        check_vma=False,
    )
```

```python
import functools

import jax
import jax.numpy as jnp
from jax import lax
from jax.experimental import pallas as pl
from jax.experimental.pallas import tpu as pltpu
from jax.sharding import PartitionSpec as P

BAND = 3


EPSILON = 1e-05


def trade(shard, axis, first):
    peers = lax.axis_size(axis)
    pairs = [(i, i + 1) for i in range(first, peers - 1, 2)]
    return lax.ppermute(shard, axis, pairs + [(high, low) for low, high in pairs])


def bring_back(shard, axis):
    peers = lax.axis_size(axis)
    return lax.ppermute(shard, axis, [(i, i - 1) for i in range(1, peers - 1)])


def is_even():
    return lax.axis_index("var") % 2 == 0


def either(even, one, two):
    return jnp.where(even, one, two), jnp.where(even, two, one)


def swap(shard, axis, bit):
    peers = lax.axis_size(axis)
    return lax.ppermute(shard, axis, [(i, i ^ bit) for i in range(peers)])


def bits_of(peers):
    return [1 << k for k in range(peers.bit_length() - 1)]


def sum_all(value, axis):
    for bit in bits_of(lax.axis_size(axis)):
        value = value + swap(value, axis, bit)
    return value


def sum_rows(partial, axis, roles, exact=None):
    for bit in bits_of(lax.axis_size(axis)):
        pairs = partial.reshape(partial.shape[0] // 2, 2, *partial.shape[1:])
        keep = jnp.where(roles[bit], pairs[:, 1], pairs[:, 0])
        give = jnp.where(roles[bit], pairs[:, 0], pairs[:, 1])
        if bit == 1 or exact is None:
            got = swap(give, axis, bit)
        else:
            rows = give.shape[1]
            near = lax.reduce_precision(give, 8, 7)
            left = (give[:, exact:] - near[:, exact:]).astype(jnp.bfloat16)
            got = jnp.concatenate([near.astype(jnp.bfloat16), left], axis=1)
            got = swap(got, axis, bit).astype(jnp.float32)
            left = got[:, rows:]
            got = got[:, :rows]
            if rows > exact:
                got = jnp.concatenate([got[:, :exact], got[:, exact:] + left], axis=1)
        partial = keep + got
    return partial[0]


GRANT = 20 << 20


def block_of(samples):
    return 512 if samples % 512 == 0 else samples


def in_hbm(array):
    return pltpu.with_memory_space_constraint(array, pltpu.HBM)


def like(shape, dtype):
    return jax.ShapeDtypeStruct(shape, dtype)


def mask_of(row):
    lanes = 128
    return jnp.transpose(jnp.broadcast_to(row.astype(jnp.float32), (lanes, row.shape[1]))) > 0.5


def head_kernel(kept, rows, dosage_ref, a_ref, b_ref, held, sems):
    samples, width = dosage_ref.shape
    edge = a_ref.shape[1]
    block = block_of(samples) // 2
    even = is_even()
    copies = []
    for k in range(samples // block):
        part = pl.ds(k * block, block)
        copy = pltpu.make_async_copy(dosage_ref.at[part, :], held.at[part, :], sems.at[k])
        copy.start()
        copies.append(copy)
    for k, copy in enumerate(copies):
        part = pl.ds(k * block, block)
        copy.wait()
        values = held[part, :]
        owners = [values[:, low : low + kept] for low in range(0, width, rows)]
        up = jnp.concatenate(owners, axis=1)
        a_ref[part, :], b_ref[part, :] = either(even, up, values[:, :edge])


def whole():
    return pl.BlockSpec(memory_space=pltpu.VMEM)


def head_pass(dosage, kept, rows):
    samples, width = dosage.shape
    edge = width // rows * kept
    half = jnp.bfloat16
    return pl.pallas_call(
        functools.partial(head_kernel, kept, rows),
        out_shape=(like((samples, edge), half),) * 2,
        in_specs=[pl.BlockSpec(memory_space=pl.ANY)],
        out_specs=(whole(),) * 2,
        scratch_shapes=[
            pltpu.VMEM((samples, width), half),
            pltpu.SemaphoreType.DMA((2 * samples // block_of(samples),)),
        ],
        compiler_params=pltpu.CompilerParams(vmem_limit_bytes=GRANT),
        name="head",
    )(in_hbm(dosage))


def moments_kernel(cuts, rows, dosage_ref, observed_ref, *refs):
    width = dosage_ref.shape[1]
    lanes = 128
    peers = width // rows
    sums_ref = refs[-1]

    @pl.when(pl.program_id(0) == 0)
    def _():
        sums_ref[...] = jnp.zeros_like(sums_ref)

    present = mask_of(observed_ref[...])
    count = jnp.sum(jnp.where(present, 1.0, 0.0), axis=0, keepdims=True)
    for low in range(0, width, lanes):
        part = slice(low, low + lanes)
        seen = jnp.where(present, dosage_ref[:, part].astype(jnp.float32), 0.0)
        sums_ref[0:1, part] += jnp.sum(seen, axis=0, keepdims=True)
        sums_ref[1:2, part] += jnp.sum(seen * seen, axis=0, keepdims=True)
        sums_ref[2:3, part] += count
    values = dosage_ref[...]
    for k, (low, high) in enumerate(cuts):
        owners = [values[:, first + low : first + high] for first in range(0, width, rows)]
        up = jnp.concatenate(owners, axis=1)
        down = values[:, low * peers : high * peers]
        refs[2 * k][...], refs[2 * k + 1][...] = either(is_even(), up, down)


def moments_pass(dosage, observed, cuts, rows):
    samples, width = dosage.shape
    block = block_of(samples)
    sizes = [(high - low) * width // rows for low, high in cuts for _ in range(2)]
    return pl.pallas_call(
        functools.partial(moments_kernel, cuts, rows),
        grid=(samples // block,),
        out_shape=tuple(like((samples, size), jnp.bfloat16) for size in sizes)
        + (like((8, width), jnp.float32),),
        in_specs=[
            pl.BlockSpec((block, width), lambda i: (i, 0)),
            pl.BlockSpec((1, block), lambda i: (0, i)),
        ],
        out_specs=tuple(pl.BlockSpec((block, size), lambda i: (i, 0)) for size in sizes)
        + (pl.BlockSpec((8, width), lambda i: (0, 0)),),
        compiler_params=pltpu.CompilerParams(vmem_limit_bytes=GRANT),
        cost_estimate=pl.CostEstimate(
            flops=8 * samples * width, bytes_accessed=4 * samples * width, transcendentals=0
        ),
        name="moments",
    )(in_hbm(dosage), observed)


def facts_kernel(cuts, rows, sums_ref, observed_ref, moments_ref, a_ref, b_ref):
    width = sums_ref.shape[1]
    totals = sums_ref[2:3, :]
    centre = sums_ref[0:1, :] / totals
    inverse = 1.0 / jnp.sqrt(sums_ref[1:2, :] / totals - centre * centre + EPSILON)
    moments_ref[0:1, :] = centre
    moments_ref[1:2, :] = inverse
    flags = observed_ref[...].astype(jnp.float32)
    even = is_even()
    cuts = [(first + low, first + high) for low, high in cuts for first in range(0, width, rows)]
    for line, natural in enumerate((centre, inverse)):
        ordered = jnp.concatenate([natural[:, low:high] for low, high in cuts], axis=1)
        one, two = either(even, ordered, natural)
        a_ref[line : line + 1, :] = one
        b_ref[line : line + 1, :] = two
    for ref in (a_ref, b_ref):
        for line in range(flags.shape[1] // width):
            ref[2 + line : 3 + line, :] = flags[:, line * width : (line + 1) * width]


def facts_pass(sums, observed, cuts, rows):
    samples, width = observed.shape[1], sums.shape[1]
    single = jnp.float32
    return pl.pallas_call(
        functools.partial(facts_kernel, cuts, rows),
        out_shape=(like((2, width), single),) + (like((2 + samples // width, width), single),) * 2,
        in_specs=[whole()] * 2,
        out_specs=(whole(),) * 3,
        compiler_params=pltpu.CompilerParams(vmem_limit_bytes=GRANT),
        name="facts",
    )(sums, observed)


def standardize(values, present, moments):
    spread = (values.astype(jnp.float32) - moments[0:1]) * moments[1:2]
    return jnp.where(present, spread, 0.0).astype(jnp.bfloat16)


def flags_in(facts, k, block):
    lines = block // facts.shape[1]
    return jnp.concatenate([facts[2 + k * lines + j : 3 + k * lines + j] for j in range(lines)], 1)


def decode(values, facts, present, first):
    parts = []
    for low in range(0, values.shape[1], present.shape[1]):
        part = slice(low, low + present.shape[1])
        place = slice(first + low, first + low + present.shape[1])
        spread = values[:, part].astype(jnp.float32) - facts[0:1, place]
        spread = spread * facts[1:2, place]
        parts.append(jnp.where(present, spread, 0.0).astype(jnp.bfloat16))
    return parts[0] if len(parts) == 1 else jnp.concatenate(parts, axis=1)


def cross(left, right):
    return lax.dot_general(
        left, right, (((0,), (0,)), ((), ())), preferred_element_type=jnp.float32
    )


def chunk_kernel(step, marks, last, observed_ref, a_ref, b_ref, a_facts, b_facts, *refs):
    lanes = 128
    olds = refs[: 2 * min(step, 1)]
    out_ref, *fresh_refs = refs[len(olds) :]
    peers = out_ref.shape[0]
    samples, _ = a_ref.shape
    old = olds[0].shape[1] if olds else 0
    block = block_of(samples)
    even = is_even()
    above_f, below_f = either(even, a_facts[...], b_facts[...])
    shares = [jnp.zeros((1, lanes), jnp.float32)] * 2
    for k in range(samples // block):
        part = slice(k * block, (k + 1) * block)
        above_present = mask_of(flags_in(above_f, k, block))
        below_present = mask_of(flags_in(below_f, k, block))
        if step == 0:
            own_present = mask_of(observed_ref[:, part])
            shares = [
                share
                + jnp.sum(jnp.where(other & above_present, 1.0, 0.0), axis=0, keepdims=True)
                for share, other in zip(shares, (own_present, below_present))
            ]
        above, below = either(even, a_ref[part, :], b_ref[part, :])
        above = decode(above, above_f, above_present, old)
        below = decode(below, below_f, below_present, old)
        if last:
            fresh_refs[0][part, :] = above
        else:
            for ref, value, earlier in zip(fresh_refs, (above, below), olds or (None, None)):
                if old:
                    ref[part, :old] = earlier[part, :]
                ref[part, old:] = value
        products = []
        if old:
            product = cross(olds[1][part, :], above)
            for low, high in zip(marks[:step], marks[1 : step + 1]):
                products.append(product[low * peers : high * peers])
            products.append(cross(below, olds[0][part, :]))
        products.append(cross(below, above))
        for owner in range(peers):
            into = out_ref.at[owner]
            low = 0
            for product in products:
                tall = product.shape[0] // peers
                for left in range(0, product.shape[1], lanes):
                    value = product[owner * tall : (owner + 1) * tall, left : left + lanes]
                    add_to(into, slice(low, low + tall), value, k)
                    low += tall
    if step == 0:
        low = out_ref.shape[1] - 8
        for owner in range(peers):
            out_ref[owner, low : low + 1, :] = shares[0]
            out_ref[owner, low + 1 : low + 2, :] = shares[1]
            out_ref[owner, low + 2 :, :] = jnp.zeros((6, lanes), jnp.float32)


def add_to(ref, part, value, step):
    ref[part, :] = value if step == 0 else ref[part, :] + value


def chunk_pass(step, marks, peers, observed, a, b, a_facts, b_facts, olds):
    samples, fresh = a.shape
    last = step == len(marks) - 2
    lanes = 128
    old = olds[0].shape[1] if olds else 0
    lines = (2 * old * fresh + fresh * fresh) // (peers * lanes) + (8 if step == 0 else 0)
    stored = like((samples, fresh if last else old + fresh), jnp.bfloat16)
    results = (like((peers, lines, lanes), jnp.float32),) + (stored,) * (1 if last else 2)
    return pl.pallas_call(
        functools.partial(chunk_kernel, step, marks, last),
        out_shape=results,
        in_specs=[whole()] * (5 + len(olds)),
        out_specs=(whole(),) * len(results),
        compiler_params=pltpu.CompilerParams(vmem_limit_bytes=GRANT),
        cost_estimate=pl.CostEstimate(
            flops=2 * samples * lines * peers * lanes,
            bytes_accessed=8 * samples * fresh,
            transcendentals=0,
        ),
    )(observed, a, b, a_facts, b_facts, *olds)


def unpack(lines, shapes):
    blocks, low = [], 0
    for tall, wide in shapes:
        pieces = []
        for _ in range(wide // lines.shape[1]):
            pieces.append(lines[low : low + tall])
            low += tall
        blocks.append(jnp.concatenate(pieces, axis=1) if len(pieces) > 1 else pieces[0])
    return blocks


def per_device(dosage, observed, band_reach):
    _, width = dosage.shape
    peers = lax.axis_size("samp")
    rows = width // peers
    marks = (0, rows // 2, 3 * rows // 4, rows)
    cuts = tuple(zip(marks[:-1], marks[1:]))
    heights = [high - low for low, high in cuts]
    wides = [height * peers for height in heights]
    a_1, b_1 = head_pass(dosage, heights[0], rows)
    a_1 = trade(a_1, "var", 0)
    b_1 = trade(b_1, "var", 1)
    place = lax.axis_index("samp")
    roles = {bit: (place & bit) != 0 for bit in bits_of(peers)}
    a_2, b_2, a_3, b_3, sums = moments_pass(dosage, observed, cuts[1:], rows)
    sums = sum_all(sums, "samp")
    moments, a_f, b_f = facts_pass(sums, observed, cuts, rows)
    a_f = trade(a_f, "var", 0)
    b_f = trade(b_f, "var", 1)
    a_2 = trade(a_2, "var", 0)
    b_2 = trade(b_2, "var", 1)
    a_3 = trade(a_3, "var", 0)
    b_3 = trade(b_3, "var", 1)
    own = standardize(dosage, (observed[0] != 0)[:, None], moments)
    own = lax.optimization_barrier(own)
    same = sum_rows(cross(own, own).reshape(peers, rows, width), "samp", roles)
    chunks = [(a_1, b_1), (a_2, b_2), (a_3, b_3)]
    products, olds, aboves = [], [], []
    for step, (a, b) in enumerate(chunks):
        product, *olds = chunk_pass(step, marks, peers, observed, a, b, a_f, b_f, olds)
        products.append(product)
        aboves.append(olds[0])
    shapes = [
        [(heights[j], wides[step]) for j in range(step)]
        + [(heights[step], wides[j]) for j in range(step + 1)]
        for step in range(3)
    ]
    shares = jnp.maximum(sum_all(products[0][0, -8:], "samp"), 1.0)
    near_0 = cross(own, aboves[0]).reshape(peers, rows, -1)
    one = jnp.concatenate([products[1], products[0][:, :-8]], axis=1)
    one = sum_rows(one, "samp", roles, one.shape[1])
    far_1 = one / shares[1:2]
    far_1 = bring_back(far_1, "var")
    near_1 = cross(own, aboves[1][:, wides[0] :]).reshape(peers, rows, -1)
    near_1 = jnp.concatenate([near_0, near_1], axis=2)
    near_1 = sum_rows(near_1, "samp", roles, rows)
    near_1 = near_1 / jnp.concatenate([shares[0:1]] * (near_1.shape[1] // 128), axis=1)
    far_2 = sum_rows(products[2], "samp", roles, products[2].shape[1]) / shares[1:2]
    far_2 = bring_back(far_2, "var")
    near_2 = cross(own, aboves[2]).reshape(peers, rows, -1)
    near_2 = sum_rows(near_2, "samp", roles, rows) / shares[0:1]
    early = unpack(far_1, shapes[1] + shapes[0])
    near = jnp.concatenate([near_1, near_2], axis=1)
    same = same / jnp.maximum(sums[2:3], 1.0)
    late = unpack(far_2, shapes[2])
    far = jnp.concatenate(
        [
            jnp.concatenate([early[3], early[0], late[0]], axis=1),
            jnp.concatenate([early[1], early[2], late[1]], axis=1),
            jnp.concatenate(late[2:], axis=1),
        ],
        axis=0,
    )
    result = jnp.stack([same, near, far], axis=1)
    keep = jnp.arange(BAND, dtype=jnp.int32) <= band_reach[0]
    return jnp.where(keep[None, :, None], result, jnp.float32(0.0))[None]


def solution(mesh):
    return jax.shard_map(
        per_device,
        mesh=mesh,
        in_specs=(P("samp", ("seg", "var")), P(("seg", "var"), "samp"), P(("seg", "var"))),
        out_specs=P(("seg", "var"), "samp", None, None),
        check_vma=False,
    )
```

```python
import functools

import jax
import jax.numpy as jnp
from jax import lax
from jax.experimental import pallas as pl
from jax.experimental.pallas import tpu as pltpu
from jax.sharding import PartitionSpec as P

BAND = 3


EPSILON = 1e-05


def trade(shard, axis, first):
    peers = lax.axis_size(axis)
    pairs = [(i, i + 1) for i in range(first, peers - 1, 2)]
    return lax.ppermute(shard, axis, pairs + [(high, low) for low, high in pairs])


def bring_back(shard, axis):
    peers = lax.axis_size(axis)
    return lax.ppermute(shard, axis, [(i, i - 1) for i in range(1, peers - 1)])


def is_even():
    return lax.axis_index("var") % 2 == 0


def either(even, one, two):
    return jnp.where(even, one, two), jnp.where(even, two, one)


def swap(shard, axis, bit):
    peers = lax.axis_size(axis)
    return lax.ppermute(shard, axis, [(i, i ^ bit) for i in range(peers)])


def bits_of(peers):
    return [1 << k for k in range(peers.bit_length() - 1)]


def sum_all(value, axis):
    for bit in bits_of(lax.axis_size(axis)):
        value = value + swap(value, axis, bit)
    return value


def sum_rows(partial, axis, roles, exact=None):
    for bit in bits_of(lax.axis_size(axis)):
        pairs = partial.reshape(partial.shape[0] // 2, 2, *partial.shape[1:])
        keep = jnp.where(roles[bit], pairs[:, 1], pairs[:, 0])
        give = jnp.where(roles[bit], pairs[:, 0], pairs[:, 1])
        if bit == 1 or exact is None:
            got = swap(give, axis, bit)
        else:
            rows = give.shape[1]
            near = lax.reduce_precision(give, 8, 7)
            left = (give[:, exact:] - near[:, exact:]).astype(jnp.bfloat16)
            got = jnp.concatenate([near.astype(jnp.bfloat16), left], axis=1)
            got = swap(got, axis, bit).astype(jnp.float32)
            left = got[:, rows:]
            got = got[:, :rows]
            if rows > exact:
                got = jnp.concatenate([got[:, :exact], got[:, exact:] + left], axis=1)
        partial = keep + got
    return partial[0]


GRANT = 20 << 20


def block_of(samples):
    return 512 if samples % 512 == 0 else samples


def in_hbm(array):
    return pltpu.with_memory_space_constraint(array, pltpu.HBM)


def like(shape, dtype):
    return jax.ShapeDtypeStruct(shape, dtype)


def mask_of(row):
    lanes = 128
    return jnp.transpose(jnp.broadcast_to(row.astype(jnp.float32), (lanes, row.shape[1]))) > 0.5


def head_kernel(kept, rows, dosage_ref, a_ref, b_ref, held, sems):
    samples, width = dosage_ref.shape
    edge = a_ref.shape[1]
    block = block_of(samples) // 2
    even = is_even()
    copies = []
    for k in range(samples // block):
        part = pl.ds(k * block, block)
        copy = pltpu.make_async_copy(dosage_ref.at[part, :], held.at[part, :], sems.at[k])
        copy.start()
        copies.append(copy)
    for k, copy in enumerate(copies):
        part = pl.ds(k * block, block)
        copy.wait()
        values = held[part, :]
        owners = [values[:, low : low + kept] for low in range(0, width, rows)]
        up = jnp.concatenate(owners, axis=1)
        a_ref[part, :], b_ref[part, :] = either(even, up, values[:, :edge])


def whole():
    return pl.BlockSpec(memory_space=pltpu.VMEM)


def head_pass(dosage, kept, rows):
    samples, width = dosage.shape
    edge = width // rows * kept
    half = jnp.bfloat16
    return pl.pallas_call(
        functools.partial(head_kernel, kept, rows),
        out_shape=(like((samples, edge), half),) * 2,
        in_specs=[pl.BlockSpec(memory_space=pl.ANY)],
        out_specs=(whole(),) * 2,
        scratch_shapes=[
            pltpu.VMEM((samples, width), half),
            pltpu.SemaphoreType.DMA((2 * samples // block_of(samples),)),
        ],
        compiler_params=pltpu.CompilerParams(vmem_limit_bytes=GRANT),
        name="head",
    )(in_hbm(dosage))


def moments_kernel(cuts, rows, dosage_ref, observed_ref, *refs):
    width = dosage_ref.shape[1]
    lanes = 128
    peers = width // rows
    sums_ref = refs[-1]

    @pl.when(pl.program_id(0) == 0)
    def _():
        sums_ref[...] = jnp.zeros_like(sums_ref)

    present = mask_of(observed_ref[...])
    count = jnp.sum(jnp.where(present, 1.0, 0.0), axis=0, keepdims=True)
    for low in range(0, width, lanes):
        part = slice(low, low + lanes)
        seen = jnp.where(present, dosage_ref[:, part].astype(jnp.float32), 0.0)
        sums_ref[0:1, part] += jnp.sum(seen, axis=0, keepdims=True)
        sums_ref[1:2, part] += jnp.sum(seen * seen, axis=0, keepdims=True)
        sums_ref[2:3, part] += count
    values = dosage_ref[...]
    for k, (low, high) in enumerate(cuts):
        owners = [values[:, first + low : first + high] for first in range(0, width, rows)]
        up = jnp.concatenate(owners, axis=1)
        down = values[:, low * peers : high * peers]
        refs[2 * k][...], refs[2 * k + 1][...] = either(is_even(), up, down)


def moments_pass(dosage, observed, cuts, rows):
    samples, width = dosage.shape
    block = block_of(samples)
    sizes = [(high - low) * width // rows for low, high in cuts for _ in range(2)]
    return pl.pallas_call(
        functools.partial(moments_kernel, cuts, rows),
        grid=(samples // block,),
        out_shape=tuple(like((samples, size), jnp.bfloat16) for size in sizes)
        + (like((8, width), jnp.float32),),
        in_specs=[
            pl.BlockSpec((block, width), lambda i: (i, 0)),
            pl.BlockSpec((1, block), lambda i: (0, i)),
        ],
        out_specs=tuple(pl.BlockSpec((block, size), lambda i: (i, 0)) for size in sizes)
        + (pl.BlockSpec((8, width), lambda i: (0, 0)),),
        compiler_params=pltpu.CompilerParams(vmem_limit_bytes=GRANT),
        cost_estimate=pl.CostEstimate(
            flops=8 * samples * width, bytes_accessed=4 * samples * width, transcendentals=0
        ),
        name="moments",
    )(in_hbm(dosage), observed)


def facts_kernel(cuts, rows, sums_ref, observed_ref, moments_ref, a_ref, b_ref):
    width = sums_ref.shape[1]
    totals = sums_ref[2:3, :]
    centre = sums_ref[0:1, :] / totals
    inverse = 1.0 / jnp.sqrt(sums_ref[1:2, :] / totals - centre * centre + EPSILON)
    moments_ref[0:1, :] = centre
    moments_ref[1:2, :] = inverse
    flags = observed_ref[...].astype(jnp.float32)
    even = is_even()
    cuts = [(first + low, first + high) for low, high in cuts for first in range(0, width, rows)]
    for line, natural in enumerate((centre, inverse)):
        ordered = jnp.concatenate([natural[:, low:high] for low, high in cuts], axis=1)
        one, two = either(even, ordered, natural)
        a_ref[line : line + 1, :] = one
        b_ref[line : line + 1, :] = two
    for ref in (a_ref, b_ref):
        for line in range(flags.shape[1] // width):
            ref[2 + line : 3 + line, :] = flags[:, line * width : (line + 1) * width]


def facts_pass(sums, observed, cuts, rows):
    samples, width = observed.shape[1], sums.shape[1]
    single = jnp.float32
    return pl.pallas_call(
        functools.partial(facts_kernel, cuts, rows),
        out_shape=(like((2, width), single),) + (like((2 + samples // width, width), single),) * 2,
        in_specs=[whole()] * 2,
        out_specs=(whole(),) * 3,
        compiler_params=pltpu.CompilerParams(vmem_limit_bytes=GRANT),
        name="facts",
    )(sums, observed)


def standardize(values, present, moments):
    spread = (values.astype(jnp.float32) - moments[0:1]) * moments[1:2]
    return jnp.where(present, spread, 0.0).astype(jnp.bfloat16)


def flags_in(facts, k, block):
    lines = block // facts.shape[1]
    return jnp.concatenate([facts[2 + k * lines + j : 3 + k * lines + j] for j in range(lines)], 1)


def decode(values, facts, present, first):
    parts = []
    for low in range(0, values.shape[1], present.shape[1]):
        part = slice(low, low + present.shape[1])
        place = slice(first + low, first + low + present.shape[1])
        spread = values[:, part].astype(jnp.float32) - facts[0:1, place]
        spread = spread * facts[1:2, place]
        parts.append(jnp.where(present, spread, 0.0).astype(jnp.bfloat16))
    return parts[0] if len(parts) == 1 else jnp.concatenate(parts, axis=1)


def cross(left, right):
    return lax.dot_general(
        left, right, (((0,), (0,)), ((), ())), preferred_element_type=jnp.float32
    )


def chunk_kernel(step, marks, last, observed_ref, a_ref, b_ref, a_facts, b_facts, *refs):
    lanes = 128
    olds = refs[: 2 * min(step, 1)]
    out_ref, *fresh_refs = refs[len(olds) :]
    peers = out_ref.shape[0]
    samples, _ = a_ref.shape
    old = olds[0].shape[1] if olds else 0
    block = block_of(samples)
    even = is_even()
    above_f, below_f = either(even, a_facts[...], b_facts[...])
    shares = [jnp.zeros((1, lanes), jnp.float32)] * 2
    for k in range(samples // block):
        part = slice(k * block, (k + 1) * block)
        above_present = mask_of(flags_in(above_f, k, block))
        below_present = mask_of(flags_in(below_f, k, block))
        if step == 0:
            own_present = mask_of(observed_ref[:, part])
            shares = [
                share
                + jnp.sum(jnp.where(other & above_present, 1.0, 0.0), axis=0, keepdims=True)
                for share, other in zip(shares, (own_present, below_present))
            ]
        above, below = either(even, a_ref[part, :], b_ref[part, :])
        above = decode(above, above_f, above_present, old)
        below = decode(below, below_f, below_present, old)
        if last:
            fresh_refs[0][part, :] = above
        else:
            for ref, value, earlier in zip(fresh_refs, (above, below), olds or (None, None)):
                if old:
                    ref[part, :old] = earlier[part, :]
                ref[part, old:] = value
        products = []
        if old:
            product = cross(olds[1][part, :], above)
            for low, high in zip(marks[:step], marks[1 : step + 1]):
                products.append(product[low * peers : high * peers])
            product = cross(below, jnp.concatenate([olds[0][part, :], above], axis=1))
            products.append(product)
        else:
            products.append(cross(below, above))
        for owner in range(peers):
            into = out_ref.at[owner]
            low = 0
            for product in products:
                tall = product.shape[0] // peers
                for left in range(0, product.shape[1], lanes):
                    value = product[owner * tall : (owner + 1) * tall, left : left + lanes]
                    add_to(into, slice(low, low + tall), value, k)
                    low += tall
    if step == 0:
        low = out_ref.shape[1] - 8
        for owner in range(peers):
            out_ref[owner, low : low + 1, :] = shares[0]
            out_ref[owner, low + 1 : low + 2, :] = shares[1]
            out_ref[owner, low + 2 :, :] = jnp.zeros((6, lanes), jnp.float32)


def add_to(ref, part, value, step):
    ref[part, :] = value if step == 0 else ref[part, :] + value


def chunk_pass(step, marks, peers, observed, a, b, a_facts, b_facts, olds):
    samples, fresh = a.shape
    last = step == len(marks) - 2
    lanes = 128
    old = olds[0].shape[1] if olds else 0
    lines = (2 * old * fresh + fresh * fresh) // (peers * lanes) + (8 if step == 0 else 0)
    stored = like((samples, fresh if last else old + fresh), jnp.bfloat16)
    results = (like((peers, lines, lanes), jnp.float32),) + (stored,) * (1 if last else 2)
    return pl.pallas_call(
        functools.partial(chunk_kernel, step, marks, last),
        out_shape=results,
        in_specs=[whole()] * (5 + len(olds)),
        out_specs=(whole(),) * len(results),
        compiler_params=pltpu.CompilerParams(vmem_limit_bytes=GRANT),
        cost_estimate=pl.CostEstimate(
            flops=2 * samples * lines * peers * lanes,
            bytes_accessed=8 * samples * fresh,
            transcendentals=0,
        ),
    )(observed, a, b, a_facts, b_facts, *olds)


def unpack(lines, shapes):
    blocks, low = [], 0
    for tall, wide in shapes:
        pieces = []
        for _ in range(wide // lines.shape[1]):
            pieces.append(lines[low : low + tall])
            low += tall
        blocks.append(jnp.concatenate(pieces, axis=1) if len(pieces) > 1 else pieces[0])
    return blocks


def per_device(dosage, observed, band_reach):
    _, width = dosage.shape
    peers = lax.axis_size("samp")
    rows = width // peers
    marks = (0, rows // 2, 3 * rows // 4, rows)
    cuts = tuple(zip(marks[:-1], marks[1:]))
    heights = [high - low for low, high in cuts]
    wides = [height * peers for height in heights]
    a_1, b_1 = head_pass(dosage, heights[0], rows)
    a_1 = trade(a_1, "var", 0)
    b_1 = trade(b_1, "var", 1)
    place = lax.axis_index("samp")
    roles = {bit: (place & bit) != 0 for bit in bits_of(peers)}
    a_2, b_2, a_3, b_3, sums = moments_pass(dosage, observed, cuts[1:], rows)
    sums = sum_all(sums, "samp")
    moments, a_f, b_f = facts_pass(sums, observed, cuts, rows)
    a_f = trade(a_f, "var", 0)
    b_f = trade(b_f, "var", 1)
    a_2 = trade(a_2, "var", 0)
    b_2 = trade(b_2, "var", 1)
    a_3 = trade(a_3, "var", 0)
    b_3 = trade(b_3, "var", 1)
    own = standardize(dosage, (observed[0] != 0)[:, None], moments)
    own = lax.optimization_barrier(own)
    same = sum_rows(cross(own, own).reshape(peers, rows, width), "samp", roles)
    chunks = [(a_1, b_1), (a_2, b_2), (a_3, b_3)]
    products, olds, aboves = [], [], []
    for step, (a, b) in enumerate(chunks):
        product, *olds = chunk_pass(step, marks, peers, observed, a, b, a_f, b_f, olds)
        products.append(product)
        aboves.append(olds[0])
    shapes = [
        [(heights[j], wides[step]) for j in range(step)]
        + [(heights[step], wides[j]) for j in range(step + 1)]
        for step in range(3)
    ]
    lines = products[1].shape[1] + products[0].shape[1] - 8
    one = jnp.concatenate([products[1], products[0]], axis=1)
    one = sum_rows(one, "samp", roles, lines)
    shares = jnp.maximum(one[lines:], 1.0)
    far_1 = one[:lines] / shares[1:2]
    far_1 = bring_back(far_1, "var")
    near_1 = cross(own, aboves[1]).reshape(peers, rows, -1)
    near_1 = sum_rows(near_1, "samp", roles, rows)
    near_1 = near_1 / jnp.concatenate([shares[0:1]] * (near_1.shape[1] // 128), axis=1)
    far_2 = sum_rows(products[2], "samp", roles, products[2].shape[1]) / shares[1:2]
    far_2 = bring_back(far_2, "var")
    near_2 = cross(own, aboves[2]).reshape(peers, rows, -1)
    near_2 = sum_rows(near_2, "samp", roles, rows) / shares[0:1]
    early = unpack(far_1, shapes[1] + shapes[0])
    near = jnp.concatenate([near_1, near_2], axis=1)
    same = same / jnp.maximum(sums[2:3], 1.0)
    late = unpack(far_2, shapes[2])
    far = jnp.concatenate(
        [
            jnp.concatenate([early[3], early[0], late[0]], axis=1),
            jnp.concatenate([early[1], early[2], late[1]], axis=1),
            jnp.concatenate(late[2:], axis=1),
        ],
        axis=0,
    )
    result = jnp.stack([same, near, far], axis=1)
    keep = jnp.arange(BAND, dtype=jnp.int32) <= band_reach[0]
    return jnp.where(keep[None, :, None], result, jnp.float32(0.0))[None]


def solution(mesh):
    return jax.shard_map(
        per_device,
        mesh=mesh,
        in_specs=(P("samp", ("seg", "var")), P(("seg", "var"), "samp"), P(("seg", "var"))),
        out_specs=P(("seg", "var"), "samp", None, None),
        check_vma=False,
    )
```
